32 devices in a mesh: seq: 16 (over z, x, core), tp: 2 (over y).
Axes of the slice: x: 2, y: 2, z: 4, core: 2. Of those that a mesh axis runs over, the one named last changes fastest.
Arguments:
- normed_input: bfloat16 [2048, 4096], P(('seq', 'tp')), may hold values from -6 to 6
- output_gradient: bfloat16 [2048, 14336], P('seq', 'tp'), may hold values from -0.75 to 0.75
- adapter_down: bfloat16 [64, 16, 4096], P('seq', None, 'tp'), may hold values from -0.09375 to 0.09375
- adapter_up: bfloat16 [64, 16, 14336], P('seq', None, 'tp'), may hold values from -1.5 to 1.5
- adapter_of_block: int32 [16], P('seq'), may hold values from 0 to 63
- live_per_block: int32 [16], P('seq'), may hold values from 32 to 128, as said below
- adapter_home_row: int32 [64], replicated, may hold values from 0 to 63, each once
Outputs:
- adapter_output: bfloat16 [2048, 14336], P('seq', 'tp')
- input_gradient: bfloat16 [2048, 4096], P(('seq', 'tp'))
- down_gradient: float32 [64, 16, 4096], P('seq', None, 'tp')
- up_gradient: float32 [64, 16, 14336], P('seq', None, 'tp')
The draws below stay inside these ranges and needn't reach their ends.
Inputs may be any that keep to these rules, and one draw needn't show every extreme that they name: `live_per_block`: every eighth block, counting from block 0, is full. `adapter_home_row`: each row appears once.
All inputs are finite; a program needn't handle non-finite values.
Results may differ from the reference program's by a relative error of at most 0.0051.
Values may be sent and summed in bfloat16 or wider, within the bound.
A program may use at most 128 MiB of HBM per device.

```python
import math
import jax
import jax.numpy as jnp
import numpy as np
from jax import lax

INPUT_FEATURES = 4096
HIDDEN_UNITS = 14336
ADAPTER_RANK = 16
ADAPTER_COUNT = 64
BLK = 128
TOKENS = 2048
NBLK = 16


def draw_live_per_block(key, part):
    spread = jax.random.randint(key, (NBLK,), BLK // 4, BLK + 1)
    full_rows = jnp.arange(NBLK) % 8 == 0
    return jnp.where(full_rows, BLK, spread).astype(jnp.int32)


def touch_ends(drawn, rng, least, top_value):
    dims = drawn.shape
    index_at = [jax.random.randint(jax.random.fold_in(rng, axis), (), 0, dims[axis]) for axis in range(len(dims))]
    drawn = drawn.at[tuple(index_at)].set(least)
    longest = dims.index(max(dims))
    index_at[longest] = (index_at[longest] + 1) % dims[longest]
    return drawn.at[tuple(index_at)].set(top_value)


def steps_of(stream_key, shape, pieces, least, largest):
    def one(axis_at, blocks):
        heights = jax.random.uniform(jax.random.fold_in(jax.random.fold_in(stream_key, 6), axis_at), (blocks,), jnp.float32, least / len(pieces), largest / len(pieces))
        return jnp.repeat(jnp.exp(heights), shape[axis_at] // blocks).reshape((-1,) + (1,) * (len(shape) - axis_at - 1))

    level = one(*pieces[0])
    for cut in pieces[1:]:
        level = level * one(*cut)
    return level


def rank_table(count, skew):
    loads = [(1 << 20) // math.isqrt(rank ** skew) + 1 for rank in range(1, count + 1)]
    deviation = 1 + sum(loads) // (1 << 30)
    return np.cumsum(np.array([max(1, weight // deviation) for weight in loads]))


def ranked_ids(stream_key, extent, amount, slope):
    table = rank_table(amount, slope)
    pick = jax.random.randint(jax.random.fold_in(stream_key, 1), extent, 0, int(table[amount - 1]))
    rank = jnp.searchsorted(jnp.asarray(table, jnp.int32), pick, side="right")
    return jax.random.permutation(jax.random.fold_in(stream_key, 2), amount)[rank].astype(jnp.int32)


def normal_values(key, shape, width, most, cuts=(), kind=jnp.bfloat16):
    values = jax.random.normal(key, shape, jnp.float32) * width
    if len(cuts) > 0:
        values = steps_of(key, shape, cuts, -0.22, 0.18) * values
    return jnp.clip(values, min=-most, max=most).astype(kind)


def setup_inputs(seed: int = 0) -> dict:
    splits = jax.random.split(jax.random.key(seed), 8)
    return {
        "normed_input": normal_values(splits[0], (TOKENS, INPUT_FEATURES), 1.0, 6.0, ((0, 32),)),
        "output_gradient": normal_values(splits[1], (TOKENS, HIDDEN_UNITS), 0.125, 0.75, ((0, 16), (1, 2))),
        "adapter_down": normal_values(splits[2], (ADAPTER_COUNT, ADAPTER_RANK, INPUT_FEATURES), INPUT_FEATURES ** -0.5, 0.09375, ((0, 16), (2, 2))),
        "adapter_up": normal_values(splits[3], (ADAPTER_COUNT, ADAPTER_RANK, HIDDEN_UNITS), ADAPTER_RANK ** -0.5, 1.5, ((0, 16), (2, 2))),
        "adapter_of_block": touch_ends(ranked_ids(splits[4], (NBLK,), ADAPTER_COUNT, 2), jax.random.fold_in(splits[4], 3), 0, ADAPTER_COUNT - 1).astype(jnp.int32),
        "live_per_block": draw_live_per_block(jax.random.fold_in(splits[7], 71), 0),
        "adapter_home_row": jax.random.permutation(splits[6], ADAPTER_COUNT).astype(jnp.int32),
    }


adapter_scale = 2.0


def reference(normed_input, output_gradient, adapter_down, adapter_up, adapter_of_block, live_per_block, adapter_home_row):
    total_blocks = adapter_of_block.shape[0]
    block_length = normed_input.shape[0] // total_blocks
    x_blocks = normed_input.reshape(total_blocks, block_length, normed_input.shape[1])
    g_blocks = output_gradient.reshape(total_blocks, block_length, output_gradient.shape[1])
    token_live_mask = (jnp.arange(block_length, dtype=jnp.int32)[None, :] < live_per_block[:, None]).astype(jnp.float32)

    def one_block(block_item):
        x_rows, gradient_rows, selected_adapter, mask_row = block_item
        down_factor = adapter_down[selected_adapter]
        up_factor = adapter_up[selected_adapter]
        mask_column = mask_row[:, None]
        down_sum = jnp.dot(x_rows, down_factor.T, preferred_element_type=jnp.float32)
        down_reduced = (down_sum * mask_column).astype(jnp.bfloat16)
        output_rows = (adapter_scale * jnp.dot(down_reduced, up_factor, preferred_element_type=jnp.float32)).astype(jnp.bfloat16)
        backward_total = jnp.dot(gradient_rows, up_factor.T, preferred_element_type=jnp.float32)
        backward_reduced = (adapter_scale * backward_total * mask_column).astype(jnp.bfloat16)
        gx_rows = jnp.dot(backward_reduced, down_factor, preferred_element_type=jnp.float32).astype(jnp.bfloat16)
        ga_part = jnp.dot(backward_reduced.T, x_rows, preferred_element_type=jnp.float32)
        up_gradient_piece = adapter_scale * jnp.dot(down_reduced.T, gradient_rows, preferred_element_type=jnp.float32)
        return output_rows, gx_rows, ga_part, up_gradient_piece

    up_output, gx_b, ga_b, gb_b = lax.map(one_block, (x_blocks, g_blocks, adapter_of_block, token_live_mask))
    token_count = adapter_down.shape[0]
    seg_a = jax.ops.segment_sum(ga_b, adapter_of_block, num_segments=token_count)
    seg_b = jax.ops.segment_sum(gb_b, adapter_of_block, num_segments=token_count)
    down_gradient = jnp.zeros_like(seg_a).at[adapter_home_row].set(seg_a)
    up_gradient = jnp.zeros_like(seg_b).at[adapter_home_row].set(seg_b)
    adapter_output = up_output.reshape(output_gradient.shape)
    input_gradient = gx_b.reshape(normed_input.shape)
    return adapter_output, input_gradient, down_gradient, up_gradient
```

```python
import functools

import jax
import jax.numpy as jnp
from jax import lax
from jax.experimental import pallas as pl
from jax.experimental.pallas import tpu as pltpu
from jax.sharding import PartitionSpec as P

adapter_scale = 2.0
GROUP = 4
MESH = pl.DeviceIdType.MESH
VMEM = pltpu.VMEM
SMEM = pltpu.SMEM

DOWN_FACTOR, UP_FACTOR = "Xx", "xxxxxxX"
UP_GRADIENT, DOWN_GRADIENT = "xzxzxzx", "XX"
LAG = 6


def pieces(width, most):
    tiles = width // 128
    count = max(k for k in range(1, most + 1) if tiles % k == 0)
    step = width // count
    return [(i * step, step) for i in range(count)]


def layout(width, hidden):
    out = []
    for which, size, most in (("a", width // 2, len(DOWN_FACTOR)), ("b", hidden // 2, len(UP_FACTOR))):
        base = 0 if which == "a" else width // 2
        for i, (start, step) in enumerate(pieces(size, most)):
            out.append((which, i, start, step, base + start))
    return out


def greet(n, tp, me, mine, partners):
    barrier = pltpu.get_barrier_semaphore()

    def signal(seq_at, tp_at):
        pl.semaphore_signal(barrier, inc=1, device_id=(seq_at, tp_at), device_id_type=MESH)

    for partner in partners:
        signal(partner, mine)
    for d in range(1, tp):
        signal(me, lax.rem(mine + d, tp))
    pl.semaphore_wait(barrier, len(partners) + tp - 1)


def step_kernel(
    n, tp, a_ref, b_ref, x_ref, g_ref, adapter_ref, live_ref, home_ref,
    out_ref, grad_a, grad_b, x_out,
    pick_a, pick_b, raw, chosen, land, far_land, fin, terms, spare, placed, xt, g, ids, part, gx,
    raw_send, raw_recv, hop_send, hop_recv, plane_send, plane_recv, fin_send, fin_recv,
    lead_send, lead_recv, go_send, pass_send, go_recv, cross_send, cross_recv, out_send, out_recv,
    id_send, id_recv, x_send, x_recv, part_send, part_recv, gx_send, gx_recv, local_sem,
):
    me, mine = lax.axis_index("seq"), lax.axis_index("tp")
    planes = n // GROUP
    p, spot = me // GROUP, lax.rem(me, GROUP)
    side, core = spot // 2, lax.rem(spot, 2)
    near_spot, far_spot = spot + 1 - 2 * core, spot + 2 - 4 * side
    diag_spot = far_spot + 1 - 2 * core
    first = p * GROUP
    near, far, diag = first + near_spot, first + far_spot, first + diag_spot
    rows = a_ref.shape[0]
    rank = pick_a.shape[0]
    width, hidden = pick_a.shape[1], pick_b.shape[1]
    half_a, half_b = width // 2, hidden // 2
    tokens = g.shape[0]
    slots = rows // rank
    f32, low = jnp.float32, jnp.bfloat16
    chunks = layout(width, hidden)
    count = len(chunks)

    def remote(src, dst, send, recv, seq_at, tp_at=mine):
        return pltpu.make_async_remote_copy(
            src_ref=src, dst_ref=dst, send_sem=send, recv_sem=recv,
            device_id=(seq_at, tp_at), device_id_type=MESH,
        )

    def at(index, step, size=None):
        return pl.ds(pl.multiple_of(index * step, step), step if size is None else size)

    def half_cols(chunk, which_half):
        which, _, start, size, _ = chunk
        half = half_a if which == "a" else half_b
        return pl.ds(pl.multiple_of(which_half * half + start, 128), size)

    def span(chunk):
        return pl.ds(chunk[4], chunk[3])

    def when(cond, body):
        if cond is True:
            body()
        else:
            pl.when(cond)(body)

    pending = []
    tick = [0]

    def send(copy, cond=True):
        copy.start()
        pending.append((tick[0], cond, copy))

    def drain(before):
        while pending and pending[0][0] < before:
            _, cond, copy = pending.pop(0)
            when(cond, copy.wait_send)

    local = [
        pltpu.make_async_copy(a_ref.at[:, at(core, half_a)], raw.at[at(spot, rows), pl.ds(0, half_a)], local_sem.at[0]),
        pltpu.make_async_copy(b_ref.at[:, at(core, half_b)], raw.at[at(spot, rows), pl.ds(half_a, half_b)], local_sem.at[1]),
        pltpu.make_async_copy(x_ref.at[:, at(mine, width)], xt.at[mine], local_sem.at[2]),
        pltpu.make_async_copy(g_ref, g, local_sem.at[3]),
    ]
    for copy in local:
        copy.start()
    adapter = adapter_ref[0]
    home = home_ref[adapter]
    id_row = lax.broadcasted_iota(jnp.int32, ids.shape[1:], 0)
    ids[me] = jnp.where(id_row == 0, adapter, home)
    others = [lax.rem(p + d, planes) for d in range(1, planes)]
    greet(n, tp, me, mine, [near, far, diag] + [q * GROUP + spot for q in others])
    for partner in (near, far, diag):
        send(remote(ids.at[me], ids.at[me], id_send.at[0], id_recv.at[planes], partner))
    pending.clear()

    factor_kind = [DOWN_FACTOR[i] if w == "a" else UP_FACTOR[i] for w, i, *_ in chunks]
    term_kind = [DOWN_GRADIENT[i] if w == "a" else UP_GRADIENT[i] for w, i, *_ in chunks]

    def x_first(kind):
        return kind in "xX"

    def relayed(kind):
        return kind in "xz"

    pairs = planes // 2
    pair = p // 2
    partner = p + 1 - 2 * lax.rem(p, 2)
    other_pairs = [lax.rem(pair + d, pairs) for d in range(1, pairs)]

    def inner(other):
        return 2 * other + (other < pair).astype(jnp.int32)

    def seat(plane):
        return plane * GROUP + spot

    def factor(chunk):
        return a_ref if chunk[0] == "a" else b_ref

    def picked(chunk):
        return pick_a if chunk[0] == "a" else pick_b

    raw_copies = {}

    def raw_out(j):
        chunk = chunks[j]
        own, sp = at(spot, rows), span(chunk)
        there, here = factor(chunk).at[:, half_cols(chunk, 1 - core)], factor(chunk).at[:, half_cols(chunk, core)]
        routes = [(there, near), (here, far), (there, diag)][:3 if x_first(factor_kind[j]) else 1]
        for src, to in routes:
            remote(src, raw.at[own, sp], raw_send.at[j], raw_recv.at[j], to).start()
        everything = raw.at[pl.ds(0, len(routes) * rows), sp]
        raw_copies[j] = remote(everything, everything, raw_send.at[j], raw_recv.at[j], near)
        pending.append((tick[0], True, raw_copies[j]))

    for j in range(min(4, count)):
        raw_out(j)
    x_copies = []
    for d in range(1, tp):
        peer = lax.rem(mine + d, tp)
        x_copies.append(remote(x_ref.at[:, at(peer, width)], xt.at[mine], x_send.at[d], x_recv.at[d], me, peer))
        x_copies[-1].start()
    for copy in local:
        copy.wait()
    plane_ids = ids.at[pl.ds(first, GROUP - 1)]
    remote(plane_ids, plane_ids, id_send.at[0], id_recv.at[planes], near).wait()

    def id_hop(source, to, sends):
        block = ids.at[at(source, GROUP)]
        return remote(block, block, sends, id_recv.at[source], to)

    for q in others:
        id_hop(p, q * GROUP + spot, id_send.at[1]).start()
    for q in others:
        id_hop(q, near, id_send.at[1]).wait_recv()
    other_ids = ids.at[pl.ds(0, GROUP * (planes - 1))]
    remote(other_ids, other_ids, id_send.at[1], id_recv.at[0], near).wait_send()

    def wanted(block, which, shape):
        return jnp.broadcast_to(ids[block, which:which + 1, 0:1], shape)

    def selector(spots, base, depth):
        shape = (rank, depth)
        row_at, col_at = lax.broadcasted_iota(jnp.int32, shape, 0), lax.broadcasted_iota(jnp.int32, shape, 1)
        found = []
        for q in range(planes):
            for s in spots:
                local_id = wanted(q * GROUP + s, 0, shape) - base
                found.append((col_at == local_id * rank + row_at).astype(f32))
        return jnp.concatenate(found, axis=0).astype(low)

    pick_x = selector([side * 2, side * 2 + 1], first * slots, GROUP * rows)
    pick_z = selector(list(range(GROUP)), (first + side * 2) * slots, 2 * rows)

    def placement(owner):
        shape = (rows, n * rank)
        row_at, col_at = lax.broadcasted_iota(jnp.int32, shape, 0), lax.broadcasted_iota(jnp.int32, shape, 1)
        target = jnp.full(shape, -1, jnp.int32)
        for block in range(n):
            begin = block * rank
            here = (wanted(block, 1, shape) - owner * slots) * rank + col_at - begin
            target = jnp.where((col_at >= begin) & (col_at < begin + rank), here, target)
        return (target == row_at).astype(f32).astype(low)

    place = jnp.concatenate([placement(me), placement(near)], axis=0)

    def factor_rows(j):
        return 2 * rank if x_first(factor_kind[j]) else GROUP * rank

    def select(j):
        sp, kind = span(chunks[j]), factor_kind[j]
        if j + 4 < count:
            raw_out(j + 4)
        raw_copies[j].wait_recv()
        if x_first(kind):
            got = jnp.dot(pick_x, raw[:, sp], preferred_element_type=f32)
        else:
            got = jnp.dot(pick_z, raw[at(side, 2 * rows), sp], preferred_element_type=f32)
        depth = factor_rows(j)
        chosen[:, pl.ds(0, depth), sp] = got.astype(low).reshape(planes, depth, got.shape[1])

    def each_plane(body):
        for v in range(planes):
            pl.when(p == v)(functools.partial(body, v))

    def beyond(v):
        return pl.ds(v + 1, planes - 1 - v) if v % 2 == 0 else pl.ds(0, v)

    def plane_copies(j, count):
        block = far_land.at[pl.ds(0, count), pl.ds(0, factor_rows(j)), span(chunks[j])]
        return remote(block, block, plane_send.at[j], plane_recv.at[j], near)

    def send_plane(j, q):
        rest, sp = pl.ds(0, factor_rows(j)), span(chunks[j])
        remote(chosen.at[q, rest, sp], far_land.at[p, rest, sp], plane_send.at[j], plane_recv.at[j], seat(q)).start()

    def hop(j):
        if not relayed(factor_kind[j]):
            for q in others:
                send_plane(j, q)
            pending.append((tick[0], True, plane_copies(j, planes - 1)))
            return
        rest, sp = pl.ds(0, factor_rows(j)), span(chunks[j])

        def copy(v):
            part_of = beyond(v)
            return remote(
                chosen.at[part_of, rest, sp], land.at[part_of, rest, sp], hop_send.at[j], hop_recv.at[j], seat(partner)
            )

        each_plane(lambda v: copy(v).start())
        for v in range(planes):
            pending.append((tick[0], p == v, copy(v)))

    def relay(j):
        if not relayed(factor_kind[j]):
            return
        rest, sp = pl.ds(0, factor_rows(j)), span(chunks[j])

        def body(v):
            got = pl.ds(v, planes - v) if v % 2 else pl.ds(0, v + 1)
            here = land.at[got, rest, sp]
            remote(here, here, hop_send.at[j], hop_recv.at[j], near).wait_recv()
            chosen[got, rest, sp] = chosen[got, rest, sp] + land[got, rest, sp]
            for q in range(v + 1, planes) if v % 2 else range(v):
                send_plane(j, q)

        each_plane(body)
        for v in range(planes):
            sent = planes - 1 - v if v % 2 else v
            if sent:
                pending.append((tick[0], p == v, plane_copies(j, sent)))

    fin_copies = {}

    def final(j):
        chunk, depth = chunks[j], factor_rows(j)
        sp = span(chunk)
        rest = pl.ds(0, depth)
        sources = [inner(other) for other in other_pairs] if relayed(factor_kind[j]) else others
        if sources:
            plane_copies(j, len(sources)).wait_recv()
            total = chosen[p, rest, sp]
            for q in sources:
                total = total + far_land[q, rest, sp]
            chosen[p, rest, sp] = total
        target = picked(chunk)
        mine_cols = half_cols(chunk, core)
        if x_first(factor_kind[j]):
            fin_copies[j] = remote(
                chosen.at[p, at(1 - core, rank), sp], target.at[:, mine_cols], fin_send.at[j], fin_recv.at[j], near
            )
            fin_copies[j].start()
            target[:, mine_cols] = chosen[p, at(core, rank), sp]
        else:
            for k, (peer, peer_spot) in enumerate(((near, near_spot), (far, far_spot), (diag, diag_spot))):
                remote(chosen.at[p, at(peer_spot, rank), sp], fin.at[k, :, sp], fin_send.at[j], fin_recv.at[j], peer).start()
            fin_copies[j] = remote(fin.at[:, :, sp], fin.at[:, :, sp], fin_send.at[j], fin_recv.at[j], near)
        pending.append((tick[0], True, fin_copies[j]))

    def settle(j):
        chunk = chunks[j]
        sp = span(chunk)
        fin_copies[j].wait_recv()
        if not x_first(factor_kind[j]):
            target = picked(chunk)
            target[:, half_cols(chunk, core)] = chosen[p, at(spot, rank), sp] + fin[1, :, sp]
            target[:, half_cols(chunk, 1 - core)] = fin[0, :, sp] + fin[2, :, sp]

    def outer(left, right):
        return lax.dot_general(left, right, (((1,), (1,)), ((), ())), preferred_element_type=f32)

    part_copies = []
    lane = lax.broadcasted_iota(jnp.int32, (1, tokens), 1)
    alive = (lane < live_ref[0]).astype(f32)

    def share(which, value):
        part[which, 0] = value
        for d in range(1, tp):
            copy = remote(
                part.at[which, 0], part.at[which, d], part_send.at[which, d], part_recv.at[which, d],
                me, lax.rem(mine + d, tp),
            )
            send(copy)
            part_copies.append(copy)

    def collect(which):
        value = part[which, 0]
        for d in range(1, tp):
            part_copies[which * (tp - 1) + d - 1].wait_recv()
            value = value + part[which, d]
        return value * alive

    lead_copies = {}

    def lead(j, left, right, scale):
        chunk = chunks[j]
        sp, own = span(chunk), at(me, rank)

        def term(which_half):
            value = jnp.dot(left, right(half_cols(chunk, which_half)), preferred_element_type=f32)
            return (scale * value if scale is not None else value).astype(low)

        spare[:, sp] = term(1 - core)
        remote(spare.at[:, sp], terms.at[own, sp], lead_send.at[j], lead_recv.at[j], near).start()
        if not x_first(term_kind[j]):
            remote(spare.at[:, sp], terms.at[own, sp], lead_send.at[j], lead_recv.at[j], diag).start()
        terms[own, sp] = term(core)
        if not x_first(term_kind[j]):
            remote(terms.at[own, sp], terms.at[own, sp], lead_send.at[j], lead_recv.at[j], far).start()
        everything = terms.at[pl.ds(0, (1 if x_first(term_kind[j]) else GROUP - 1) * rank), sp]
        lead_copies[j] = remote(everything, everything, lead_send.at[j], lead_recv.at[j], near)
        pending.append((tick[0], True, lead_copies[j]))

    def group_rows(j, plane, other_side=False):
        if not x_first(term_kind[j]):
            return at(plane, GROUP * rank)
        return at(plane * 2 + (1 - side if other_side else side), 2 * rank)

    def term_copy(j, plane, sends, to):
        block = terms.at[group_rows(j, plane), span(chunks[j])]
        return remote(block, block, sends.at[j], go_recv.at[j, plane], to)

    def cross_copy(j, plane):
        block = terms.at[group_rows(j, plane), span(chunks[j])]
        return remote(block, block, cross_send.at[j], cross_recv.at[j], far)

    def crossed(j):
        everything = terms.at[pl.ds(0, planes * 2 * rank), span(chunks[j])]
        return remote(everything, everything, cross_send.at[j], cross_recv.at[j], far)

    def spread(j):
        lead_copies[j].wait_recv()
        targets = [partner] + [inner(other) for other in other_pairs] if relayed(term_kind[j]) else others
        for q in targets:
            term_copy(j, p, go_send, seat(q)).start()
        if x_first(term_kind[j]):
            cross_copy(j, p).start()
        pending.append((tick[0], True, term_copies(j, go_send, len(targets))))

    def term_copies(j, sends, number):
        block = terms.at[pl.ds(0, number * (2 if x_first(term_kind[j]) else GROUP) * rank), span(chunks[j])]
        return remote(block, block, sends.at[j], go_recv.at[j, 0], near)

    def arrive(j, q):
        term_copy(j, q, go_send, near).wait_recv()
        if x_first(term_kind[j]):
            cross_copy(j, q).start()

    def pass_on(j):
        if not relayed(term_kind[j]):
            for q in others:
                arrive(j, q)
            return
        arrive(j, partner)

        def body(v):
            for q in range(v) if v % 2 == 0 else range(planes - 1, v, -1):
                term_copy(j, q, go_send, near).wait_recv()
                term_copy(j, q, pass_send, seat(partner)).start()
                if x_first(term_kind[j]):
                    cross_copy(j, q).start()

        each_plane(body)
        for v in range(planes):
            passed = v if v % 2 == 0 else planes - 1 - v
            if passed:
                pending.append((tick[0], p == v, term_copies(j, pass_send, passed)))

    def gather(j):
        if relayed(term_kind[j]):

            def body(v):
                for q in range(v + 2, planes) if v % 2 == 0 else range(v - 2, -1, -1):
                    arrive(j, q)

            each_plane(body)
        if x_first(term_kind[j]):
            pending.append((tick[0], True, crossed(j)))

    out_copies = {}

    def finish(j):
        chunk = chunks[j]
        sp, cols = span(chunk), half_cols(chunk, core)
        if x_first(term_kind[j]):
            crossed(j).wait_recv()
        out = grad_a if chunk[0] == "a" else grad_b
        total = jnp.dot(place, terms[:, sp], preferred_element_type=f32)
        placed[:, sp] = total[rows:]
        out_copies[j] = remote(placed.at[:, sp], out.at[:, cols], out_send.at[j], out_recv.at[j], near)
        send(out_copies[j])
        out[:, cols] = total[:rows]

    state = {}

    def start_down():
        for copy in x_copies:
            copy.wait()
        share(0, outer(pick_a[...], xt[...].reshape(tokens, width)))

    def finish_down():
        down = collect(0).astype(low)
        state["down"] = down
        state["down_t"] = down.T

    def add_back(j):
        total = state.get("back")
        for h in (core, 1 - core):
            cols = half_cols(chunks[j], h)
            value = outer(pick_b[:, cols], g[:, cols])
            total = value if total is None else total + value
        state["back"] = total

    def output(j):
        for h in (core, 1 - core):
            cols = half_cols(chunks[j], h)
            value = jnp.dot(state["down_t"], pick_b[:, cols], preferred_element_type=f32)
            out_ref[:, cols] = (adapter_scale * value).astype(low)

    def start_back():
        share(1, state["back"])

    gx_copies = []

    def finish_back():
        back = adapter_scale * collect(1)
        state["back_low"] = back.astype(low)
        state["back_t"] = back.T.astype(low)

    def input_gradient():
        gx[...] = jnp.dot(state["back_t"], pick_a[...], preferred_element_type=f32).astype(low).reshape(gx.shape)
        for d in range(1, tp):
            peer = lax.rem(mine + d, tp)
            gx_copies.append(remote(gx.at[peer], x_out.at[:, at(mine, width)], gx_send.at[d], gx_recv.at[d], me, peer))
            gx_copies[-1].start()
        x_out[:, at(mine, width)] = gx[mine]

    events = []

    def plan(when_at, order, body):
        events.append((when_at, order, len(events), body))

    downs = [j for j in range(count) if chunks[j][0] == "a"]
    ups = [j for j in range(count) if chunks[j][0] == "b"]
    for j in range(count):
        plan(j, 5, functools.partial(select, j))
        plan(j, 5, functools.partial(hop, j))
        plan(j + 1, 4, functools.partial(relay, j))
        plan(j + 2, 3, functools.partial(final, j))
        plan(j + 3, 2, functools.partial(settle, j))
        if j in ups:
            plan(j + 3, 2, functools.partial(add_back, j))
    ready = downs[-1] + 3
    plan(ready, 2, start_down)
    plan(ready + 1, 1, finish_down)

    def chain(j, begin, left, right, scale):
        plan(begin, 6, lambda: lead(j, state[left], right, scale))
        plan(begin + 1, 7, functools.partial(spread, j))
        plan(begin + 2, 8, functools.partial(pass_on, j))
        plan(begin + 3, 9, functools.partial(gather, j))
        plan(begin + 4, 10, functools.partial(finish, j))

    for i, j in enumerate(ups):
        plan(max(ready + 1, j + 3) + 2, 11, functools.partial(output, j))
        chain(j, ready + 1 + i, "down", lambda cols: g[:, cols], adapter_scale)
    whole = ups[-1] + 3
    plan(whole, 2, start_back)
    plan(whole + 1, 1, finish_back)
    for i, j in enumerate(downs):
        chain(j, whole + 1, "back_low", lambda cols: xt[:, :, cols].reshape(tokens, cols.size), None)
    plan(whole + 1, 12, input_gradient)
    for when_at, _, _, body in sorted(events, key=lambda event: event[:3]):
        if when_at != tick[0]:
            tick[0] = when_at
            drain(when_at - LAG)
        body()
    for j in ups + downs:
        out_copies[j].wait_recv()
    for copy in gx_copies:
        copy.wait()
    drain(tick[0] + 1)


def step(n, tp, a, b, x, g, adapter, live, home):
    slots, rank, width = a.shape
    hidden = b.shape[2]
    rows = x.shape[0]
    tokens = g.shape[0]
    planes = n // GROUP
    cuts = len(layout(width, hidden))
    own = slots * rank
    each = (width + hidden) // 2
    low, f32 = jnp.bfloat16, jnp.float32
    dma = pltpu.SemaphoreType.DMA
    hbm = pl.BlockSpec(memory_space=pltpu.HBM)
    inside = pl.BlockSpec(memory_space=VMEM)
    scalar = pl.BlockSpec(memory_space=SMEM)
    lists = [dma((cuts,)) for _ in range(12)]
    results = ((tokens, hidden), low), ((own, width), f32), ((own, hidden), f32), ((rows, tp * width), low)
    held = pl.pallas_call(
        functools.partial(step_kernel, n, tp),
        out_shape=tuple(VMEM(*result) for result in results),
        in_specs=[hbm] * 4 + [scalar] * 3,
        out_specs=(inside,) * 4,
        scratch_shapes=[
            VMEM((rank, width), low), VMEM((rank, hidden), low), VMEM((GROUP * own, each), low),
            VMEM((planes, GROUP * rank, each), low),
            VMEM((planes, GROUP * rank, each), low), VMEM((planes, GROUP * rank, each), low),
            VMEM((3, rank, each), low), VMEM((n * rank, each), low), VMEM((rank, each), low), VMEM((own, each), f32),
            VMEM((tp, rows, width), low), VMEM((tokens, hidden), low),
            VMEM((n, 2, 128), jnp.int32), VMEM((2, tp, rank, tokens), f32), VMEM((tp, rows, width), low),
            *lists, dma((cuts, planes)), dma((cuts,)), dma((cuts,)), dma((cuts,)), dma((cuts,)),
            dma((3,)), dma((planes + 1,)), dma((tp,)), dma((tp,)), dma((2, tp)), dma((2, tp)),
            dma((tp,)), dma((tp,)), dma((4,)),
        ],
        compiler_params=pltpu.CompilerParams(
            collective_id=0, has_side_effects=True, vmem_limit_bytes=56 * 1024 * 1024
        ),
    )(a.reshape(own, width), b.reshape(own, hidden), x, g, adapter, live, home)
    return held


def per_device(
    normed_input,
    output_gradient,
    adapter_down,
    adapter_up,
    adapter_of_block,
    live_per_block,
    adapter_home_row,
):
    n, tp = lax.axis_size("seq"), lax.axis_size("tp")
    slots, rank, width = adapter_down.shape
    hidden = adapter_up.shape[2]
    out, grad_a, grad_b, gx = step(
        n, tp, adapter_down, adapter_up, normed_input, output_gradient,
        adapter_of_block, live_per_block, adapter_home_row,
    )
    return (out, gx, grad_a.reshape(slots, rank, width), grad_b.reshape(slots, rank, hidden))


def solution(mesh):
    placed = (
        P(("seq", "tp"), None),
        P("seq", "tp"),
        P("seq", None, "tp"),
        P("seq", None, "tp"),
        P("seq"),
        P("seq"),
        P(),
    )
    return jax.shard_map(
        per_device,
        mesh=mesh,
        in_specs=placed,
        out_specs=(
            P("seq", "tp"),
            P(("seq", "tp"), None),
            P("seq", None, "tp"),
            P("seq", None, "tp"),
        ),
        check_vma=False,
    )
```

```python
import functools

import jax
import jax.numpy as jnp
from jax import lax
from jax.experimental import pallas as pl
from jax.experimental.pallas import tpu as pltpu
from jax.sharding import PartitionSpec as P

adapter_scale = 2.0
GROUP = 4
MESH = pl.DeviceIdType.MESH
VMEM = pltpu.VMEM
SMEM = pltpu.SMEM

DOWN_FACTOR, UP_FACTOR = "XX", "xxxxxxX"
UP_GRADIENT, DOWN_GRADIENT = "xxxxxxX", "XZ"
RELAY, LAND, NEAR, SHARE, LEAD, SPREAD, CROSS = 2, 2, 1, 1, 1, 2, 1
AHEAD, LAG = 4, 6


def pieces(width, most):
    tiles = width // 128
    count = max(k for k in range(1, most + 1) if tiles % k == 0)
    step = width // count
    return [(i * step, step) for i in range(count)]


def layout(width, hidden):
    out = []
    for which, size, most in (("a", width // 2, len(DOWN_FACTOR)), ("b", hidden // 2, len(UP_FACTOR))):
        base = 0 if which == "a" else width // 2
        for i, (start, step) in enumerate(pieces(size, most)):
            out.append((which, i, start, step, base + start))
    return out


def greet(n, tp, me, mine, partners):
    barrier = pltpu.get_barrier_semaphore()

    def signal(seq_at, tp_at):
        pl.semaphore_signal(barrier, inc=1, device_id=(seq_at, tp_at), device_id_type=MESH)

    for partner in partners:
        signal(partner, mine)
    for d in range(1, tp):
        signal(me, lax.rem(mine + d, tp))
    pl.semaphore_wait(barrier, len(partners) + tp - 1)


def step_kernel(
    n, tp, a_ref, b_ref, x_ref, g_ref, adapter_ref, live_ref, home_ref,
    out_ref, grad_a, grad_b, x_out,
    pick_a, pick_b, raw, chosen, land, far_land, fin, terms, spare, placed, xt, g, ids, part, gx,
    raw_send, raw_recv, hop_send, hop_recv, plane_send, plane_recv, fin_send, fin_recv,
    lead_send, lead_recv, go_send, pass_send, go_recv, cross_send, cross_recv, out_send, out_recv,
    id_send, id_recv, x_send, x_recv, part_send, part_recv, gx_send, gx_recv, local_sem,
):
    me, mine = lax.axis_index("seq"), lax.axis_index("tp")
    planes = n // GROUP
    p, spot = me // GROUP, lax.rem(me, GROUP)
    side, core = spot // 2, lax.rem(spot, 2)
    near_spot, far_spot = spot + 1 - 2 * core, spot + 2 - 4 * side
    diag_spot = far_spot + 1 - 2 * core
    first = p * GROUP
    near, far, diag = first + near_spot, first + far_spot, first + diag_spot
    rows = a_ref.shape[0]
    rank = pick_a.shape[0]
    width, hidden = pick_a.shape[1], pick_b.shape[1]
    half_a, half_b = width // 2, hidden // 2
    tokens = g.shape[0]
    slots = rows // rank
    f32, low = jnp.float32, jnp.bfloat16
    chunks = layout(width, hidden)
    count = len(chunks)

    def remote(src, dst, send, recv, seq_at, tp_at=mine):
        return pltpu.make_async_remote_copy(
            src_ref=src, dst_ref=dst, send_sem=send, recv_sem=recv,
            device_id=(seq_at, tp_at), device_id_type=MESH,
        )

    def at(index, step, size=None):
        return pl.ds(pl.multiple_of(index * step, step), step if size is None else size)

    def half_cols(chunk, which_half):
        which, _, start, size, _ = chunk
        half = half_a if which == "a" else half_b
        return pl.ds(pl.multiple_of(which_half * half + start, 128), size)

    def span(chunk):
        return pl.ds(chunk[4], chunk[3])

    def when(cond, body):
        if cond is True:
            body()
        else:
            pl.when(cond)(body)

    pending = []
    tick = [0]

    def send(copy, cond=True):
        copy.start()
        pending.append((tick[0], cond, copy))

    def drain(before):
        while pending and pending[0][0] < before:
            _, cond, copy = pending.pop(0)
            when(cond, copy.wait_send)

    local = [
        pltpu.make_async_copy(a_ref.at[:, at(core, half_a)], raw.at[at(spot, rows), pl.ds(0, half_a)], local_sem.at[0]),
        pltpu.make_async_copy(b_ref.at[:, at(core, half_b)], raw.at[at(spot, rows), pl.ds(half_a, half_b)], local_sem.at[1]),
        pltpu.make_async_copy(x_ref.at[:, at(mine, width)], xt.at[mine], local_sem.at[2]),
        pltpu.make_async_copy(g_ref, g, local_sem.at[3]),
    ]
    for copy in local:
        copy.start()
    adapter = adapter_ref[0]
    home = home_ref[adapter]
    id_row = lax.broadcasted_iota(jnp.int32, ids.shape[1:], 0)
    ids[me] = jnp.where(id_row == 0, adapter, home)
    others = [lax.rem(p + d, planes) for d in range(1, planes)]
    greet(n, tp, me, mine, [near, far, diag] + [q * GROUP + spot for q in others])
    for partner in (near, far, diag):
        send(remote(ids.at[me], ids.at[me], id_send.at[0], id_recv.at[planes], partner))
    pending.clear()

    factor_kind = [DOWN_FACTOR[i] if w == "a" else UP_FACTOR[i] for w, i, *_ in chunks]
    term_kind = [DOWN_GRADIENT[i] if w == "a" else UP_GRADIENT[i] for w, i, *_ in chunks]

    def x_first(kind):
        return kind in "xX"

    def relayed(kind):
        return kind in "xz"

    pairs = planes // 2
    pair = p // 2
    partner = p + 1 - 2 * lax.rem(p, 2)
    other_pairs = [lax.rem(pair + d, pairs) for d in range(1, pairs)]

    def inner(other):
        return 2 * other + (other < pair).astype(jnp.int32)

    def seat(plane):
        return plane * GROUP + spot

    def factor(chunk):
        return a_ref if chunk[0] == "a" else b_ref

    def picked(chunk):
        return pick_a if chunk[0] == "a" else pick_b

    raw_copies = {}

    def raw_out(j):
        chunk = chunks[j]
        own, sp = at(spot, rows), span(chunk)
        there, here = factor(chunk).at[:, half_cols(chunk, 1 - core)], factor(chunk).at[:, half_cols(chunk, core)]
        routes = [(there, near), (here, far), (there, diag)][:3 if x_first(factor_kind[j]) else 1]
        for src, to in routes:
            remote(src, raw.at[own, sp], raw_send.at[j], raw_recv.at[j], to).start()
        everything = raw.at[pl.ds(0, len(routes) * rows), sp]
        raw_copies[j] = remote(everything, everything, raw_send.at[j], raw_recv.at[j], near)
        pending.append((tick[0], True, raw_copies[j]))

    for j in range(min(AHEAD, count)):
        raw_out(j)
    x_copies = []
    for d in range(1, tp):
        peer = lax.rem(mine + d, tp)
        x_copies.append(remote(x_ref.at[:, at(peer, width)], xt.at[mine], x_send.at[d], x_recv.at[d], me, peer))
        x_copies[-1].start()
    for copy in local:
        copy.wait()
    plane_ids = ids.at[pl.ds(first, GROUP - 1)]
    remote(plane_ids, plane_ids, id_send.at[0], id_recv.at[planes], near).wait()

    def id_hop(source, to, sends):
        block = ids.at[at(source, GROUP)]
        return remote(block, block, sends, id_recv.at[source], to)

    for q in others:
        id_hop(p, q * GROUP + spot, id_send.at[1]).start()
    for q in others:
        id_hop(q, near, id_send.at[1]).wait_recv()
    other_ids = ids.at[pl.ds(0, GROUP * (planes - 1))]
    remote(other_ids, other_ids, id_send.at[1], id_recv.at[0], near).wait_send()

    def wanted(block, which, shape):
        return jnp.broadcast_to(ids[block, which:which + 1, 0:1], shape)

    def selector(spots, base, depth):
        shape = (rank, depth)
        row_at, col_at = lax.broadcasted_iota(jnp.int32, shape, 0), lax.broadcasted_iota(jnp.int32, shape, 1)
        found = []
        for q in range(planes):
            for s in spots:
                local_id = wanted(q * GROUP + s, 0, shape) - base
                found.append((col_at == local_id * rank + row_at).astype(f32))
        return jnp.concatenate(found, axis=0).astype(low)

    pick_x = selector([side * 2, side * 2 + 1], first * slots, GROUP * rows)
    pick_z = selector(list(range(GROUP)), (first + side * 2) * slots, 2 * rows)

    def placement(owner):
        shape = (rows, n * rank)
        row_at, col_at = lax.broadcasted_iota(jnp.int32, shape, 0), lax.broadcasted_iota(jnp.int32, shape, 1)
        target = jnp.full(shape, -1, jnp.int32)
        for block in range(n):
            begin = block * rank
            here = (wanted(block, 1, shape) - owner * slots) * rank + col_at - begin
            target = jnp.where((col_at >= begin) & (col_at < begin + rank), here, target)
        return (target == row_at).astype(f32).astype(low)

    place = jnp.concatenate([placement(me), placement(near)], axis=0)

    def factor_rows(j):
        return 2 * rank if x_first(factor_kind[j]) else GROUP * rank

    def select(j):
        sp, kind = span(chunks[j]), factor_kind[j]
        if j + AHEAD < count:
            raw_out(j + AHEAD)
        raw_copies[j].wait_recv()
        if x_first(kind):
            got = jnp.dot(pick_x, raw[:, sp], preferred_element_type=f32)
        else:
            got = jnp.dot(pick_z, raw[at(side, 2 * rows), sp], preferred_element_type=f32)
        depth = factor_rows(j)
        chosen[:, pl.ds(0, depth), sp] = got.astype(low).reshape(planes, depth, got.shape[1])

    def each_plane(body):
        for v in range(planes):
            pl.when(p == v)(functools.partial(body, v))

    def beyond(v):
        return pl.ds(v + 1, planes - 1 - v) if v % 2 == 0 else pl.ds(0, v)

    def plane_copies(j, count):
        block = far_land.at[pl.ds(0, count), pl.ds(0, factor_rows(j)), span(chunks[j])]
        return remote(block, block, plane_send.at[j], plane_recv.at[j], near)

    def send_plane(j, q):
        rest, sp = pl.ds(0, factor_rows(j)), span(chunks[j])
        remote(chosen.at[q, rest, sp], far_land.at[p, rest, sp], plane_send.at[j], plane_recv.at[j], seat(q)).start()

    def hop(j):
        if not relayed(factor_kind[j]):
            for q in others:
                send_plane(j, q)
            pending.append((tick[0], True, plane_copies(j, planes - 1)))
            return
        rest, sp = pl.ds(0, factor_rows(j)), span(chunks[j])

        def copy(v):
            part_of = beyond(v)
            return remote(
                chosen.at[part_of, rest, sp], land.at[part_of, rest, sp], hop_send.at[j], hop_recv.at[j], seat(partner)
            )

        each_plane(lambda v: copy(v).start())
        for v in range(planes):
            pending.append((tick[0], p == v, copy(v)))

    def relay(j):
        if not relayed(factor_kind[j]):
            return
        rest, sp = pl.ds(0, factor_rows(j)), span(chunks[j])

        def body(v):
            got = pl.ds(v, planes - v) if v % 2 else pl.ds(0, v + 1)
            here = land.at[got, rest, sp]
            remote(here, here, hop_send.at[j], hop_recv.at[j], near).wait_recv()
            chosen[got, rest, sp] = chosen[got, rest, sp] + land[got, rest, sp]
            for q in range(v + 1, planes) if v % 2 else range(v):
                send_plane(j, q)

        each_plane(body)
        for v in range(planes):
            sent = planes - 1 - v if v % 2 else v
            if sent:
                pending.append((tick[0], p == v, plane_copies(j, sent)))

    fin_copies = {}

    def final(j):
        chunk, depth = chunks[j], factor_rows(j)
        sp = span(chunk)
        rest = pl.ds(0, depth)
        sources = [inner(other) for other in other_pairs] if relayed(factor_kind[j]) else others
        if sources:
            plane_copies(j, len(sources)).wait_recv()
            total = chosen[p, rest, sp]
            for q in sources:
                total = total + far_land[q, rest, sp]
            chosen[p, rest, sp] = total
        target = picked(chunk)
        mine_cols = half_cols(chunk, core)
        if x_first(factor_kind[j]):
            fin_copies[j] = remote(
                chosen.at[p, at(1 - core, rank), sp], target.at[:, mine_cols], fin_send.at[j], fin_recv.at[j], near
            )
            fin_copies[j].start()
            target[:, mine_cols] = chosen[p, at(core, rank), sp]
        else:
            for k, (peer, peer_spot) in enumerate(((near, near_spot), (far, far_spot), (diag, diag_spot))):
                remote(chosen.at[p, at(peer_spot, rank), sp], fin.at[k, :, sp], fin_send.at[j], fin_recv.at[j], peer).start()
            fin_copies[j] = remote(fin.at[:, :, sp], fin.at[:, :, sp], fin_send.at[j], fin_recv.at[j], near)
        pending.append((tick[0], True, fin_copies[j]))

    def settle(j):
        chunk = chunks[j]
        sp = span(chunk)
        fin_copies[j].wait_recv()
        if not x_first(factor_kind[j]):
            target = picked(chunk)
            target[:, half_cols(chunk, core)] = chosen[p, at(spot, rank), sp] + fin[1, :, sp]
            target[:, half_cols(chunk, 1 - core)] = fin[0, :, sp] + fin[2, :, sp]

    def outer(left, right):
        return lax.dot_general(left, right, (((1,), (1,)), ((), ())), preferred_element_type=f32)

    part_copies = []
    lane = lax.broadcasted_iota(jnp.int32, (1, tokens), 1)
    alive = (lane < live_ref[0]).astype(f32)

    def share(which, value):
        part[which, 0] = value
        for d in range(1, tp):
            copy = remote(
                part.at[which, 0], part.at[which, d], part_send.at[which, d], part_recv.at[which, d],
                me, lax.rem(mine + d, tp),
            )
            send(copy)
            part_copies.append(copy)

    def collect(which):
        value = part[which, 0]
        for d in range(1, tp):
            part_copies[which * (tp - 1) + d - 1].wait_recv()
            value = value + part[which, d]
        return value * alive

    lead_copies = {}

    def lead(j, left, right, scale):
        chunk = chunks[j]
        sp, own = span(chunk), at(me, rank)

        def term(which_half):
            value = jnp.dot(left, right(half_cols(chunk, which_half)), preferred_element_type=f32)
            return (scale * value if scale is not None else value).astype(low)

        spare[:, sp] = term(1 - core)
        remote(spare.at[:, sp], terms.at[own, sp], lead_send.at[j], lead_recv.at[j], near).start()
        if not x_first(term_kind[j]):
            remote(spare.at[:, sp], terms.at[own, sp], lead_send.at[j], lead_recv.at[j], diag).start()
        terms[own, sp] = term(core)
        if not x_first(term_kind[j]):
            remote(terms.at[own, sp], terms.at[own, sp], lead_send.at[j], lead_recv.at[j], far).start()
        everything = terms.at[pl.ds(0, (1 if x_first(term_kind[j]) else GROUP - 1) * rank), sp]
        lead_copies[j] = remote(everything, everything, lead_send.at[j], lead_recv.at[j], near)
        pending.append((tick[0], True, lead_copies[j]))

    def group_rows(j, plane, other_side=False):
        if not x_first(term_kind[j]):
            return at(plane, GROUP * rank)
        return at(plane * 2 + (1 - side if other_side else side), 2 * rank)

    def term_copy(j, plane, sends, to):
        block = terms.at[group_rows(j, plane), span(chunks[j])]
        return remote(block, block, sends.at[j], go_recv.at[j, plane], to)

    def cross_copy(j, plane):
        block = terms.at[group_rows(j, plane), span(chunks[j])]
        return remote(block, block, cross_send.at[j], cross_recv.at[j], far)

    def crossed(j):
        everything = terms.at[pl.ds(0, planes * 2 * rank), span(chunks[j])]
        return remote(everything, everything, cross_send.at[j], cross_recv.at[j], far)

    def spread(j):
        lead_copies[j].wait_recv()
        targets = [partner] + [inner(other) for other in other_pairs] if relayed(term_kind[j]) else others
        for q in targets:
            term_copy(j, p, go_send, seat(q)).start()
        if x_first(term_kind[j]):
            cross_copy(j, p).start()
        pending.append((tick[0], True, term_copies(j, go_send, len(targets))))

    def term_copies(j, sends, number):
        block = terms.at[pl.ds(0, number * (2 if x_first(term_kind[j]) else GROUP) * rank), span(chunks[j])]
        return remote(block, block, sends.at[j], go_recv.at[j, 0], near)

    def arrive(j, q):
        term_copy(j, q, go_send, near).wait_recv()
        if x_first(term_kind[j]):
            cross_copy(j, q).start()

    def pass_on(j):
        if not relayed(term_kind[j]):
            for q in others:
                arrive(j, q)
            return
        arrive(j, partner)

        def body(v):
            for q in range(v) if v % 2 == 0 else range(planes - 1, v, -1):
                term_copy(j, q, go_send, near).wait_recv()
                term_copy(j, q, pass_send, seat(partner)).start()
                if x_first(term_kind[j]):
                    cross_copy(j, q).start()

        each_plane(body)
        for v in range(planes):
            passed = v if v % 2 == 0 else planes - 1 - v
            if passed:
                pending.append((tick[0], p == v, term_copies(j, pass_send, passed)))

    def gather(j):
        if relayed(term_kind[j]):

            def body(v):
                for q in range(v + 2, planes) if v % 2 == 0 else range(v - 2, -1, -1):
                    arrive(j, q)

            each_plane(body)
        if x_first(term_kind[j]):
            pending.append((tick[0], True, crossed(j)))

    out_copies = {}

    def finish(j):
        chunk = chunks[j]
        sp, cols = span(chunk), half_cols(chunk, core)
        if x_first(term_kind[j]):
            crossed(j).wait_recv()
        out = grad_a if chunk[0] == "a" else grad_b
        total = jnp.dot(place, terms[:, sp], preferred_element_type=f32)
        placed[:, sp] = total[rows:]
        out_copies[j] = remote(placed.at[:, sp], out.at[:, cols], out_send.at[j], out_recv.at[j], near)
        send(out_copies[j])
        out[:, cols] = total[:rows]

    state = {}

    def start_down():
        for copy in x_copies:
            copy.wait()
        share(0, outer(pick_a[...], xt[...].reshape(tokens, width)))

    def finish_down():
        down = collect(0).astype(low)
        state["down"] = down
        state["down_t"] = down.T

    def add_back(j):
        total = state.get("back")
        for h in (core, 1 - core):
            cols = half_cols(chunks[j], h)
            value = outer(pick_b[:, cols], g[:, cols])
            total = value if total is None else total + value
        state["back"] = total

    def output(j):
        for h in (core, 1 - core):
            cols = half_cols(chunks[j], h)
            value = jnp.dot(state["down_t"], pick_b[:, cols], preferred_element_type=f32)
            out_ref[:, cols] = (adapter_scale * value).astype(low)

    def start_back():
        share(1, state["back"])

    gx_copies = []

    def finish_back():
        back = adapter_scale * collect(1)
        state["back_low"] = back.astype(low)
        state["back_t"] = back.T.astype(low)

    def input_gradient():
        gx[...] = jnp.dot(state["back_t"], pick_a[...], preferred_element_type=f32).astype(low).reshape(gx.shape)
        for d in range(1, tp):
            peer = lax.rem(mine + d, tp)
            gx_copies.append(remote(gx.at[peer], x_out.at[:, at(mine, width)], gx_send.at[d], gx_recv.at[d], me, peer))
            gx_copies[-1].start()
        x_out[:, at(mine, width)] = gx[mine]

    events = []

    def plan(when_at, order, body):
        events.append((when_at, order, len(events), body))

    downs = [j for j in range(count) if chunks[j][0] == "a"]
    ups = [j for j in range(count) if chunks[j][0] == "b"]
    def settled_at(j):
        return j + (RELAY + LAND if relayed(factor_kind[j]) else LAND) + NEAR

    for j in range(count):
        plan(j, 5, functools.partial(select, j))
        plan(j, 5, functools.partial(hop, j))
        plan(j + RELAY, 4, functools.partial(relay, j))
        plan(settled_at(j) - NEAR, 3, functools.partial(final, j))
        plan(settled_at(j), 2, functools.partial(settle, j))
        if j in ups:
            plan(settled_at(j), 2, functools.partial(add_back, j))
    ready = max(settled_at(j) for j in downs)
    plan(ready, 2, start_down)
    plan(ready + SHARE, 1, finish_down)

    def chain(j, begin, left, right, scale):
        plan(begin, 6, lambda: lead(j, state[left], right, scale))
        arrived = begin + LEAD + SPREAD
        plan(begin + LEAD, 7, functools.partial(spread, j))
        plan(arrived, 8, functools.partial(pass_on, j))
        if relayed(term_kind[j]):
            arrived += SPREAD
        plan(arrived, 9, functools.partial(gather, j))
        if x_first(term_kind[j]):
            arrived += CROSS
        plan(arrived, 10, functools.partial(finish, j))

    for i, j in enumerate(ups):
        plan(max(ready + SHARE, settled_at(j)) + 2, 11, functools.partial(output, j))
        chain(j, ready + SHARE + i, "down", lambda cols: g[:, cols], adapter_scale)
    whole = max(settled_at(j) for j in ups)
    plan(whole, 2, start_back)
    plan(whole + SHARE, 1, finish_back)
    for i, j in enumerate(downs):
        chain(j, whole + SHARE, "back_low", lambda cols: xt[:, :, cols].reshape(tokens, cols.size), None)
    plan(whole + SHARE, 12, input_gradient)
    for when_at, _, _, body in sorted(events, key=lambda event: event[:3]):
        if when_at != tick[0]:
            tick[0] = when_at
            drain(when_at - LAG)
        body()
    for j in ups + downs:
        out_copies[j].wait_recv()
    for copy in gx_copies:
        copy.wait()
    drain(tick[0] + 1)


def step(n, tp, a, b, x, g, adapter, live, home):
    slots, rank, width = a.shape
    hidden = b.shape[2]
    rows = x.shape[0]
    tokens = g.shape[0]
    planes = n // GROUP
    cuts = len(layout(width, hidden))
    own = slots * rank
    each = (width + hidden) // 2
    low, f32 = jnp.bfloat16, jnp.float32
    dma = pltpu.SemaphoreType.DMA
    hbm = pl.BlockSpec(memory_space=pltpu.HBM)
    inside = pl.BlockSpec(memory_space=VMEM)
    scalar = pl.BlockSpec(memory_space=SMEM)
    lists = [dma((cuts,)) for _ in range(12)]
    results = ((tokens, hidden), low), ((own, width), f32), ((own, hidden), f32), ((rows, tp * width), low)
    held = pl.pallas_call(
        functools.partial(step_kernel, n, tp),
        out_shape=tuple(VMEM(*result) for result in results),
        in_specs=[hbm] * 4 + [scalar] * 3,
        out_specs=(inside,) * 4,
        scratch_shapes=[
            VMEM((rank, width), low), VMEM((rank, hidden), low), VMEM((GROUP * own, each), low),
            VMEM((planes, GROUP * rank, each), low),
            VMEM((planes, GROUP * rank, each), low), VMEM((planes, GROUP * rank, each), low),
            VMEM((3, rank, each), low), VMEM((n * rank, each), low), VMEM((rank, each), low), VMEM((own, each), f32),
            VMEM((tp, rows, width), low), VMEM((tokens, hidden), low),
            VMEM((n, 2, 128), jnp.int32), VMEM((2, tp, rank, tokens), f32), VMEM((tp, rows, width), low),
            *lists, dma((cuts, planes)), dma((cuts,)), dma((cuts,)), dma((cuts,)), dma((cuts,)),
            dma((3,)), dma((planes + 1,)), dma((tp,)), dma((tp,)), dma((2, tp)), dma((2, tp)),
            dma((tp,)), dma((tp,)), dma((4,)),
        ],
        compiler_params=pltpu.CompilerParams(
            collective_id=0, has_side_effects=True, vmem_limit_bytes=56 * 1024 * 1024
        ),
    )(a.reshape(own, width), b.reshape(own, hidden), x, g, adapter, live, home)
    return held


def per_device(
    normed_input,
    output_gradient,
    adapter_down,
    adapter_up,
    adapter_of_block,
    live_per_block,
    adapter_home_row,
):
    n, tp = lax.axis_size("seq"), lax.axis_size("tp")
    slots, rank, width = adapter_down.shape
    hidden = adapter_up.shape[2]
    out, grad_a, grad_b, gx = step(
        n, tp, adapter_down, adapter_up, normed_input, output_gradient,
        adapter_of_block, live_per_block, adapter_home_row,
    )
    return (out, gx, grad_a.reshape(slots, rank, width), grad_b.reshape(slots, rank, hidden))


def solution(mesh):
    placed = (
        P(("seq", "tp"), None),
        P("seq", "tp"),
        P("seq", None, "tp"),
        P("seq", None, "tp"),
        P("seq"),
        P("seq"),
        P(),
    )
    return jax.shard_map(
        per_device,
        mesh=mesh,
        in_specs=placed,
        out_specs=(
            P("seq", "tp"),
            P(("seq", "tp"), None),
            P("seq", None, "tp"),
            P("seq", None, "tp"),
        ),
        check_vma=False,
    )
```

```python
import functools

import jax
import jax.numpy as jnp
from jax import lax
from jax.experimental import pallas as pl
from jax.experimental.pallas import tpu as pltpu
from jax.sharding import PartitionSpec as P

adapter_scale = 2.0
GROUP = 4
MESH = pl.DeviceIdType.MESH
VMEM = pltpu.VMEM
SMEM = pltpu.SMEM

DOWN_FACTOR, UP_FACTOR = "XX", "xxxxxxX"
UP_GRADIENT, DOWN_GRADIENT = "xxxxxxX", "XZ"
RELAY, LAND, NEAR, SHARE, LEAD, SPREAD, CROSS = 2, 2, 1, 1, 1, 2, 1
AHEAD, LAG = 4, 45
SCHEDULE = ()


def pieces(width, most):
    tiles = width // 128
    count = max(k for k in range(1, most + 1) if tiles % k == 0)
    step = width // count
    return [(i * step, step) for i in range(count)]


def layout(width, hidden):
    out = []
    for which, size, most in (("a", width // 2, len(DOWN_FACTOR)), ("b", hidden // 2, len(UP_FACTOR))):
        base = 0 if which == "a" else width // 2
        for i, (start, step) in enumerate(pieces(size, most)):
            out.append((which, i, start, step, base + start))
    return out


def greet(n, tp, me, mine, partners):
    barrier = pltpu.get_barrier_semaphore()

    def signal(seq_at, tp_at):
        pl.semaphore_signal(barrier, inc=1, device_id=(seq_at, tp_at), device_id_type=MESH)

    for partner in partners:
        signal(partner, mine)
    for d in range(1, tp):
        signal(me, lax.rem(mine + d, tp))
    pl.semaphore_wait(barrier, len(partners) + tp - 1)


def step_kernel(
    n, tp, a_ref, b_ref, x_ref, g_ref, adapter_ref, live_ref, home_ref,
    out_ref, grad_a, grad_b, x_out,
    pick_a, pick_b, raw, chosen, land, far_land, fin, terms, spare, placed, xt, g, ids, part, gx,
    raw_send, raw_recv, hop_send, hop_recv, plane_send, plane_recv, fin_send, fin_recv,
    lead_send, lead_recv, go_send, pass_send, go_recv, cross_send, cross_recv, out_send, out_recv,
    id_send, id_recv, x_send, x_recv, part_send, part_recv, gx_send, gx_recv, local_sem,
):
    me, mine = lax.axis_index("seq"), lax.axis_index("tp")
    planes = n // GROUP
    p, spot = me // GROUP, lax.rem(me, GROUP)
    side, core = spot // 2, lax.rem(spot, 2)
    near_spot, far_spot = spot + 1 - 2 * core, spot + 2 - 4 * side
    diag_spot = far_spot + 1 - 2 * core
    first = p * GROUP
    near, far, diag = first + near_spot, first + far_spot, first + diag_spot
    rows = a_ref.shape[0]
    rank = pick_a.shape[0]
    width, hidden = pick_a.shape[1], pick_b.shape[1]
    half_a, half_b = width // 2, hidden // 2
    tokens = g.shape[0]
    slots = rows // rank
    f32, low = jnp.float32, jnp.bfloat16
    chunks = layout(width, hidden)
    count = len(chunks)

    def remote(src, dst, send, recv, seq_at, tp_at=mine):
        return pltpu.make_async_remote_copy(
            src_ref=src, dst_ref=dst, send_sem=send, recv_sem=recv,
            device_id=(seq_at, tp_at), device_id_type=MESH,
        )

    def at(index, step, size=None):
        return pl.ds(pl.multiple_of(index * step, step), step if size is None else size)

    def half_cols(chunk, which_half):
        which, _, start, size, _ = chunk
        half = half_a if which == "a" else half_b
        return pl.ds(pl.multiple_of(which_half * half + start, 128), size)

    def span(chunk):
        return pl.ds(chunk[4], chunk[3])

    def when(cond, body):
        if cond is True:
            body()
        else:
            pl.when(cond)(body)

    pending = []
    tick = [0]

    def send(copy, cond=True):
        copy.start()
        pending.append((tick[0], cond, copy))

    def drain(before):
        while pending and pending[0][0] < before:
            _, cond, copy = pending.pop(0)
            when(cond, copy.wait_send)

    local = [
        pltpu.make_async_copy(a_ref.at[:, at(core, half_a)], raw.at[at(spot, rows), pl.ds(0, half_a)], local_sem.at[0]),
        pltpu.make_async_copy(b_ref.at[:, at(core, half_b)], raw.at[at(spot, rows), pl.ds(half_a, half_b)], local_sem.at[1]),
        pltpu.make_async_copy(x_ref.at[:, at(mine, width)], xt.at[mine], local_sem.at[2]),
        pltpu.make_async_copy(g_ref, g, local_sem.at[3]),
    ]
    for copy in local:
        copy.start()
    adapter = adapter_ref[0]
    home = home_ref[adapter]
    id_row = lax.broadcasted_iota(jnp.int32, ids.shape[1:], 0)
    ids[me] = jnp.where(id_row == 0, adapter, home)
    others = [lax.rem(p + d, planes) for d in range(1, planes)]
    greet(n, tp, me, mine, [near, far, diag] + [q * GROUP + spot for q in others])
    for partner in (near, far, diag):
        send(remote(ids.at[me], ids.at[me], id_send.at[0], id_recv.at[planes], partner))
    pending.clear()

    factor_kind = [DOWN_FACTOR[i] if w == "a" else UP_FACTOR[i] for w, i, *_ in chunks]
    term_kind = [DOWN_GRADIENT[i] if w == "a" else UP_GRADIENT[i] for w, i, *_ in chunks]

    def x_first(kind):
        return kind in "xX"

    def relayed(kind):
        return kind in "xz"

    pairs = planes // 2
    pair = p // 2
    partner = p + 1 - 2 * lax.rem(p, 2)
    other_pairs = [lax.rem(pair + d, pairs) for d in range(1, pairs)]

    def inner(other):
        return 2 * other + (other < pair).astype(jnp.int32)

    def seat(plane):
        return plane * GROUP + spot

    def factor(chunk):
        return a_ref if chunk[0] == "a" else b_ref

    def picked(chunk):
        return pick_a if chunk[0] == "a" else pick_b

    raw_copies = {}

    def raw_out(j):
        chunk = chunks[j]
        own, sp = at(spot, rows), span(chunk)
        there, here = factor(chunk).at[:, half_cols(chunk, 1 - core)], factor(chunk).at[:, half_cols(chunk, core)]
        routes = [(there, near), (here, far), (there, diag)][:3 if x_first(factor_kind[j]) else 1]
        for src, to in routes:
            remote(src, raw.at[own, sp], raw_send.at[j], raw_recv.at[j], to).start()
        everything = raw.at[pl.ds(0, len(routes) * rows), sp]
        raw_copies[j] = remote(everything, everything, raw_send.at[j], raw_recv.at[j], near)
        pending.append((tick[0], True, raw_copies[j]))

    for j in range(min(AHEAD, count)):
        raw_out(j)
    x_copies = []
    for d in range(1, tp):
        peer = lax.rem(mine + d, tp)
        x_copies.append(remote(x_ref.at[:, at(peer, width)], xt.at[mine], x_send.at[d], x_recv.at[d], me, peer))
        x_copies[-1].start()
    for copy in local:
        copy.wait()
    plane_ids = ids.at[pl.ds(first, GROUP - 1)]
    remote(plane_ids, plane_ids, id_send.at[0], id_recv.at[planes], near).wait()

    def id_hop(source, to, sends):
        block = ids.at[at(source, GROUP)]
        return remote(block, block, sends, id_recv.at[source], to)

    for q in others:
        id_hop(p, q * GROUP + spot, id_send.at[1]).start()
    for q in others:
        id_hop(q, near, id_send.at[1]).wait_recv()
    other_ids = ids.at[pl.ds(0, GROUP * (planes - 1))]
    remote(other_ids, other_ids, id_send.at[1], id_recv.at[0], near).wait_send()

    def wanted(block, which, shape):
        return jnp.broadcast_to(ids[block, which:which + 1, 0:1], shape)

    def selector(spots, base, depth):
        shape = (rank, depth)
        row_at, col_at = lax.broadcasted_iota(jnp.int32, shape, 0), lax.broadcasted_iota(jnp.int32, shape, 1)
        found = []
        for q in range(planes):
            for s in spots:
                local_id = wanted(q * GROUP + s, 0, shape) - base
                found.append((col_at == local_id * rank + row_at).astype(f32))
        return jnp.concatenate(found, axis=0).astype(low)

    pick_x = selector([side * 2, side * 2 + 1], first * slots, GROUP * rows)
    pick_z = selector(list(range(GROUP)), (first + side * 2) * slots, 2 * rows)

    def placement(owner):
        shape = (rows, n * rank)
        row_at, col_at = lax.broadcasted_iota(jnp.int32, shape, 0), lax.broadcasted_iota(jnp.int32, shape, 1)
        target = jnp.full(shape, -1, jnp.int32)
        for block in range(n):
            begin = block * rank
            here = (wanted(block, 1, shape) - owner * slots) * rank + col_at - begin
            target = jnp.where((col_at >= begin) & (col_at < begin + rank), here, target)
        return (target == row_at).astype(f32).astype(low)

    place = jnp.concatenate([placement(me), placement(near)], axis=0)

    def factor_rows(j):
        return 2 * rank if x_first(factor_kind[j]) else GROUP * rank

    def select(j):
        sp, kind = span(chunks[j]), factor_kind[j]
        if j + AHEAD < count:
            raw_out(j + AHEAD)
        raw_copies[j].wait_recv()
        if x_first(kind):
            got = jnp.dot(pick_x, raw[:, sp], preferred_element_type=f32)
        else:
            got = jnp.dot(pick_z, raw[at(side, 2 * rows), sp], preferred_element_type=f32)
        depth = factor_rows(j)
        chosen[:, pl.ds(0, depth), sp] = got.astype(low).reshape(planes, depth, got.shape[1])

    def each_plane(body):
        for v in range(planes):
            pl.when(p == v)(functools.partial(body, v))

    def beyond(v):
        return pl.ds(v + 1, planes - 1 - v) if v % 2 == 0 else pl.ds(0, v)

    def plane_copies(j, count):
        block = far_land.at[pl.ds(0, count), pl.ds(0, factor_rows(j)), span(chunks[j])]
        return remote(block, block, plane_send.at[j], plane_recv.at[j], near)

    def send_plane(j, q):
        rest, sp = pl.ds(0, factor_rows(j)), span(chunks[j])
        remote(chosen.at[q, rest, sp], far_land.at[p, rest, sp], plane_send.at[j], plane_recv.at[j], seat(q)).start()

    def hop(j):
        if not relayed(factor_kind[j]):
            for q in others:
                send_plane(j, q)
            pending.append((tick[0], True, plane_copies(j, planes - 1)))
            return
        rest, sp = pl.ds(0, factor_rows(j)), span(chunks[j])

        def copy(v):
            part_of = beyond(v)
            return remote(
                chosen.at[part_of, rest, sp], land.at[part_of, rest, sp], hop_send.at[j], hop_recv.at[j], seat(partner)
            )

        each_plane(lambda v: copy(v).start())
        for v in range(planes):
            pending.append((tick[0], p == v, copy(v)))

    def relay(j):
        if not relayed(factor_kind[j]):
            return
        rest, sp = pl.ds(0, factor_rows(j)), span(chunks[j])

        def body(v):
            got = pl.ds(v, planes - v) if v % 2 else pl.ds(0, v + 1)
            here = land.at[got, rest, sp]
            remote(here, here, hop_send.at[j], hop_recv.at[j], near).wait_recv()
            chosen[got, rest, sp] = chosen[got, rest, sp] + land[got, rest, sp]
            for q in range(v + 1, planes) if v % 2 else range(v):
                send_plane(j, q)

        each_plane(body)
        for v in range(planes):
            sent = planes - 1 - v if v % 2 else v
            if sent:
                pending.append((tick[0], p == v, plane_copies(j, sent)))

    fin_copies = {}

    def final(j):
        chunk, depth = chunks[j], factor_rows(j)
        sp = span(chunk)
        rest = pl.ds(0, depth)
        sources = [inner(other) for other in other_pairs] if relayed(factor_kind[j]) else others
        if sources:
            plane_copies(j, len(sources)).wait_recv()
            total = chosen[p, rest, sp]
            for q in sources:
                total = total + far_land[q, rest, sp]
            chosen[p, rest, sp] = total
        target = picked(chunk)
        mine_cols = half_cols(chunk, core)
        if x_first(factor_kind[j]):
            fin_copies[j] = remote(
                chosen.at[p, at(1 - core, rank), sp], target.at[:, mine_cols], fin_send.at[j], fin_recv.at[j], near
            )
            fin_copies[j].start()
            target[:, mine_cols] = chosen[p, at(core, rank), sp]
        else:
            for k, (peer, peer_spot) in enumerate(((near, near_spot), (far, far_spot), (diag, diag_spot))):
                remote(chosen.at[p, at(peer_spot, rank), sp], fin.at[k, :, sp], fin_send.at[j], fin_recv.at[j], peer).start()
            fin_copies[j] = remote(fin.at[:, :, sp], fin.at[:, :, sp], fin_send.at[j], fin_recv.at[j], near)
        pending.append((tick[0], True, fin_copies[j]))

    def settle(j):
        chunk = chunks[j]
        sp = span(chunk)
        fin_copies[j].wait_recv()
        if not x_first(factor_kind[j]):
            target = picked(chunk)
            target[:, half_cols(chunk, core)] = chosen[p, at(spot, rank), sp] + fin[1, :, sp]
            target[:, half_cols(chunk, 1 - core)] = fin[0, :, sp] + fin[2, :, sp]

    def outer(left, right):
        return lax.dot_general(left, right, (((1,), (1,)), ((), ())), preferred_element_type=f32)

    part_copies = []
    lane = lax.broadcasted_iota(jnp.int32, (1, tokens), 1)
    alive = (lane < live_ref[0]).astype(f32)

    def share(which, value):
        part[which, 0] = value
        for d in range(1, tp):
            copy = remote(
                part.at[which, 0], part.at[which, d], part_send.at[which, d], part_recv.at[which, d],
                me, lax.rem(mine + d, tp),
            )
            send(copy)
            part_copies.append(copy)

    def collect(which):
        value = part[which, 0]
        for d in range(1, tp):
            part_copies[which * (tp - 1) + d - 1].wait_recv()
            value = value + part[which, d]
        return value * alive

    lead_copies = {}

    def lead(j, left, right, scale):
        chunk = chunks[j]
        sp, own = span(chunk), at(me, rank)

        def term(which_half):
            value = jnp.dot(left, right(half_cols(chunk, which_half)), preferred_element_type=f32)
            return (scale * value if scale is not None else value).astype(low)

        spare[:, sp] = term(1 - core)
        remote(spare.at[:, sp], terms.at[own, sp], lead_send.at[j], lead_recv.at[j], near).start()
        if not x_first(term_kind[j]):
            remote(spare.at[:, sp], terms.at[own, sp], lead_send.at[j], lead_recv.at[j], diag).start()
        terms[own, sp] = term(core)
        if not x_first(term_kind[j]):
            remote(terms.at[own, sp], terms.at[own, sp], lead_send.at[j], lead_recv.at[j], far).start()
        everything = terms.at[pl.ds(0, (1 if x_first(term_kind[j]) else GROUP - 1) * rank), sp]
        lead_copies[j] = remote(everything, everything, lead_send.at[j], lead_recv.at[j], near)
        pending.append((tick[0], True, lead_copies[j]))

    def group_rows(j, plane, other_side=False):
        if not x_first(term_kind[j]):
            return at(plane, GROUP * rank)
        return at(plane * 2 + (1 - side if other_side else side), 2 * rank)

    def term_copy(j, plane, sends, to):
        block = terms.at[group_rows(j, plane), span(chunks[j])]
        return remote(block, block, sends.at[j], go_recv.at[j, plane], to)

    def cross_copy(j, plane):
        block = terms.at[group_rows(j, plane), span(chunks[j])]
        return remote(block, block, cross_send.at[j], cross_recv.at[j], far)

    def crossed(j):
        everything = terms.at[pl.ds(0, planes * 2 * rank), span(chunks[j])]
        return remote(everything, everything, cross_send.at[j], cross_recv.at[j], far)

    def spread(j):
        lead_copies[j].wait_recv()
        targets = [partner] + [inner(other) for other in other_pairs] if relayed(term_kind[j]) else others
        for q in targets:
            term_copy(j, p, go_send, seat(q)).start()
        if x_first(term_kind[j]):
            cross_copy(j, p).start()
        pending.append((tick[0], True, term_copies(j, go_send, len(targets))))

    def term_copies(j, sends, number):
        block = terms.at[pl.ds(0, number * (2 if x_first(term_kind[j]) else GROUP) * rank), span(chunks[j])]
        return remote(block, block, sends.at[j], go_recv.at[j, 0], near)

    def arrive(j, q):
        term_copy(j, q, go_send, near).wait_recv()
        if x_first(term_kind[j]):
            cross_copy(j, q).start()

    def pass_on(j):
        if not relayed(term_kind[j]):
            for q in others:
                arrive(j, q)
            return
        arrive(j, partner)

        def body(v):
            for q in range(v) if v % 2 == 0 else range(planes - 1, v, -1):
                term_copy(j, q, go_send, near).wait_recv()
                term_copy(j, q, pass_send, seat(partner)).start()
                if x_first(term_kind[j]):
                    cross_copy(j, q).start()

        each_plane(body)
        for v in range(planes):
            passed = v if v % 2 == 0 else planes - 1 - v
            if passed:
                pending.append((tick[0], p == v, term_copies(j, pass_send, passed)))

    def gather(j):
        if relayed(term_kind[j]):

            def body(v):
                for q in range(v + 2, planes) if v % 2 == 0 else range(v - 2, -1, -1):
                    arrive(j, q)

            each_plane(body)
        if x_first(term_kind[j]):
            pending.append((tick[0], True, crossed(j)))

    out_copies = {}

    def finish(j):
        chunk = chunks[j]
        sp, cols = span(chunk), half_cols(chunk, core)
        if x_first(term_kind[j]):
            crossed(j).wait_recv()
        out = grad_a if chunk[0] == "a" else grad_b
        total = jnp.dot(place, terms[:, sp], preferred_element_type=f32)
        placed[:, sp] = total[rows:]
        out_copies[j] = remote(placed.at[:, sp], out.at[:, cols], out_send.at[j], out_recv.at[j], near)
        send(out_copies[j])
        out[:, cols] = total[:rows]

    state = {}

    def start_down():
        for copy in x_copies:
            copy.wait()
        share(0, outer(pick_a[...], xt[...].reshape(tokens, width)))

    def finish_down():
        down = collect(0).astype(low)
        state["down"] = down
        state["down_t"] = down.T

    def add_back(j):
        total = state.get("back")
        for h in (core, 1 - core):
            cols = half_cols(chunks[j], h)
            value = outer(pick_b[:, cols], g[:, cols])
            total = value if total is None else total + value
        state["back"] = total

    def output(j):
        for h in (core, 1 - core):
            cols = half_cols(chunks[j], h)
            value = jnp.dot(state["down_t"], pick_b[:, cols], preferred_element_type=f32)
            out_ref[:, cols] = (adapter_scale * value).astype(low)

    def start_back():
        share(1, state["back"])

    gx_copies = []

    def finish_back():
        back = adapter_scale * collect(1)
        state["back_low"] = back.astype(low)
        state["back_t"] = back.T.astype(low)

    def input_gradient():
        gx[...] = jnp.dot(state["back_t"], pick_a[...], preferred_element_type=f32).astype(low).reshape(gx.shape)
        for d in range(1, tp):
            peer = lax.rem(mine + d, tp)
            gx_copies.append(remote(gx.at[peer], x_out.at[:, at(mine, width)], gx_send.at[d], gx_recv.at[d], me, peer))
            gx_copies[-1].start()
        x_out[:, at(mine, width)] = gx[mine]

    events = []

    def plan(when_at, order, body, stage, j=0):
        events.append((when_at, order, len(events), stage * 100 + j, body))

    downs = [j for j in range(count) if chunks[j][0] == "a"]
    ups = [j for j in range(count) if chunks[j][0] == "b"]
    def settled_at(j):
        return j + (RELAY + LAND if relayed(factor_kind[j]) else LAND) + NEAR

    for j in range(count):
        plan(j, 5, functools.partial(select, j), 0, j)
        plan(j, 5, functools.partial(hop, j), 1, j)
        plan(j + RELAY, 4, functools.partial(relay, j), 2, j)
        plan(settled_at(j) - NEAR, 3, functools.partial(final, j), 3, j)
        plan(settled_at(j), 2, functools.partial(settle, j), 4, j)
        if j in ups:
            plan(settled_at(j), 2, functools.partial(add_back, j), 5, j)
    ready = max(settled_at(j) for j in downs)
    plan(ready, 2, start_down, 12)
    plan(ready + SHARE, 1, finish_down, 13)

    def chain(j, begin, left, right, scale):
        plan(begin, 6, lambda: lead(j, state[left], right, scale), 6, j)
        arrived = begin + LEAD + SPREAD
        plan(begin + LEAD, 7, functools.partial(spread, j), 7, j)
        plan(arrived, 8, functools.partial(pass_on, j), 8, j)
        if relayed(term_kind[j]):
            arrived += SPREAD
        plan(arrived, 9, functools.partial(gather, j), 9, j)
        if x_first(term_kind[j]):
            arrived += CROSS
        plan(arrived, 10, functools.partial(finish, j), 10, j)

    for i, j in enumerate(ups):
        plan(max(ready + SHARE, settled_at(j)) + 2, 11, functools.partial(output, j), 11, j)
        chain(j, ready + SHARE + i, "down", lambda cols: g[:, cols], adapter_scale)
    whole = max(settled_at(j) for j in ups)
    plan(whole, 2, start_back, 14)
    plan(whole + SHARE, 1, finish_back, 15)
    for i, j in enumerate(downs):
        chain(j, whole + SHARE, "back_low", lambda cols: xt[:, :, cols].reshape(tokens, cols.size), None)
    plan(whole + SHARE, 12, input_gradient, 16)
    rank_of = {code: i for i, code in enumerate(SCHEDULE)}
    if set(rank_of) == {event[3] for event in events}:
        events.sort(key=lambda event: rank_of[event[3]])
    else:
        events.sort(key=lambda event: event[:3])
    for i, event in enumerate(events):
        tick[0] = i
        drain(i - LAG)
        event[4]()
    for j in ups + downs:
        out_copies[j].wait_recv()
    for copy in gx_copies:
        copy.wait()
    drain(tick[0] + 1)


def step(n, tp, a, b, x, g, adapter, live, home):
    slots, rank, width = a.shape
    hidden = b.shape[2]
    rows = x.shape[0]
    tokens = g.shape[0]
    planes = n // GROUP
    cuts = len(layout(width, hidden))
    own = slots * rank
    each = (width + hidden) // 2
    low, f32 = jnp.bfloat16, jnp.float32
    dma = pltpu.SemaphoreType.DMA
    hbm = pl.BlockSpec(memory_space=pltpu.HBM)
    inside = pl.BlockSpec(memory_space=VMEM)
    scalar = pl.BlockSpec(memory_space=SMEM)
    lists = [dma((cuts,)) for _ in range(12)]
    results = ((tokens, hidden), low), ((own, width), f32), ((own, hidden), f32), ((rows, tp * width), low)
    held = pl.pallas_call(
        functools.partial(step_kernel, n, tp),
        out_shape=tuple(VMEM(*result) for result in results),
        in_specs=[hbm] * 4 + [scalar] * 3,
        out_specs=(inside,) * 4,
        scratch_shapes=[
            VMEM((rank, width), low), VMEM((rank, hidden), low), VMEM((GROUP * own, each), low),
            VMEM((planes, GROUP * rank, each), low),
            VMEM((planes, GROUP * rank, each), low), VMEM((planes, GROUP * rank, each), low),
            VMEM((3, rank, each), low), VMEM((n * rank, each), low), VMEM((rank, each), low), VMEM((own, each), f32),
            VMEM((tp, rows, width), low), VMEM((tokens, hidden), low),
            VMEM((n, 2, 128), jnp.int32), VMEM((2, tp, rank, tokens), f32), VMEM((tp, rows, width), low),
            *lists, dma((cuts, planes)), dma((cuts,)), dma((cuts,)), dma((cuts,)), dma((cuts,)),
            dma((3,)), dma((planes + 1,)), dma((tp,)), dma((tp,)), dma((2, tp)), dma((2, tp)),
            dma((tp,)), dma((tp,)), dma((4,)),
        ],
        compiler_params=pltpu.CompilerParams(
            collective_id=0, has_side_effects=True, vmem_limit_bytes=56 * 1024 * 1024
        ),
    )(a.reshape(own, width), b.reshape(own, hidden), x, g, adapter, live, home)
    anywhere = pl.BlockSpec(memory_space=pl.ANY)
    return pl.pallas_call(
        store_kernel,
        out_shape=tuple(jax.ShapeDtypeStruct(*result) for result in results),
        in_specs=[inside] * len(results),
        out_specs=(anywhere,) * len(results),
        scratch_shapes=[dma((len(results),))],
        compiler_params=pltpu.CompilerParams(vmem_limit_bytes=1024 * 1024),
    )(*[pltpu.with_memory_space_constraint(value, VMEM) for value in held])


def store_kernel(*refs):
    sems = refs[-1]
    number = len(refs) // 2
    copies = [pltpu.make_async_copy(refs[i], refs[number + i], sems.at[i]) for i in range(number)]
    for copy in copies:
        copy.start()
    for copy in copies:
        copy.wait()


def per_device(
    normed_input,
    output_gradient,
    adapter_down,
    adapter_up,
    adapter_of_block,
    live_per_block,
    adapter_home_row,
):
    n, tp = lax.axis_size("seq"), lax.axis_size("tp")
    slots, rank, width = adapter_down.shape
    hidden = adapter_up.shape[2]
    out, grad_a, grad_b, gx = step(
        n, tp, adapter_down, adapter_up, normed_input, output_gradient,
        adapter_of_block, live_per_block, adapter_home_row,
    )
    return (out, gx, grad_a.reshape(slots, rank, width), grad_b.reshape(slots, rank, hidden))


def solution(mesh):
    placed = (
        P(("seq", "tp"), None),
        P("seq", "tp"),
        P("seq", None, "tp"),
        P("seq", None, "tp"),
        P("seq"),
        P("seq"),
        P(),
    )
    return jax.shard_map(
        per_device,
        mesh=mesh,
        in_specs=placed,
        out_specs=(
            P("seq", "tp"),
            P(("seq", "tp"), None),
            P("seq", None, "tp"),
            P("seq", None, "tp"),
        ),
        check_vma=False,
    )
```

```python
import functools

import jax
import jax.numpy as jnp
from jax import lax
from jax.experimental import pallas as pl
from jax.experimental.pallas import tpu as pltpu
from jax.sharding import PartitionSpec as P

adapter_scale = 2.0
GROUP = 4
MESH = pl.DeviceIdType.MESH
VMEM = pltpu.VMEM
SMEM = pltpu.SMEM

DOWN_FACTOR, UP_FACTOR = "XX", "xxzXxxx"
UP_GRADIENT, DOWN_GRADIENT = "xxxxxxX", "XZ"
DOWN_SHARES, UP_SHARES = (4, 4), (5, 4, 2, 4, 5, 5, 3)
RELAY, LAND, NEAR, SHARE, LEAD, SPREAD, CROSS = 2, 2, 1, 1, 1, 2, 2
AHEAD, LAG, PACE = 5, 45, 5
STORES = 1


def pieces(width, shares):
    tiles, total, seen, start, out = width // 128, sum(shares), 0, 0, []
    for i, share in enumerate(shares):
        seen += share
        end = (2 * seen * tiles + total) // (2 * total)
        if end > start:
            out.append((i, start * 128, (end - start) * 128))
        start = end
    return out


def layout(width, hidden):
    halves = ("a", 0, width // 2, DOWN_SHARES), ("b", width // 2, hidden // 2, UP_SHARES)
    return [
        (which, i, start, size, base + start)
        for which, base, half, shares in halves for i, start, size in pieces(half, shares)
    ]


def greet(n, tp, me, mine, partners):
    barrier = pltpu.get_barrier_semaphore()

    def signal(seq_at, tp_at):
        pl.semaphore_signal(barrier, inc=1, device_id=(seq_at, tp_at), device_id_type=MESH)

    for partner in partners:
        signal(partner, mine)
    for d in range(1, tp):
        signal(me, lax.rem(mine + d, tp))
    pl.semaphore_wait(barrier, len(partners) + tp - 1)


def step_kernel(
    n, tp, a_ref, b_ref, x_ref, g_ref, adapter_ref, live_ref, home_ref,
    out_ref, grad_a, grad_b, x_out,
    pick_a, pick_b, raw, chosen, land, far_land, fin, terms, spare, placed, xt, g, ids, part, gx,
    raw_send, raw_recv, hop_send, hop_recv, plane_send, plane_recv, fin_send, fin_recv,
    lead_send, lead_recv, go_send, pass_send, go_recv, cross_send, cross_recv, out_send, out_recv,
    id_send, id_recv, x_send, x_recv, part_send, part_recv, gx_send, gx_recv, local_sem,
):
    me, mine = lax.axis_index("seq"), lax.axis_index("tp")
    planes = n // GROUP
    p, spot = me // GROUP, lax.rem(me, GROUP)
    side, core = spot // 2, lax.rem(spot, 2)
    near_spot, far_spot = spot + 1 - 2 * core, spot + 2 - 4 * side
    diag_spot = far_spot + 1 - 2 * core
    first = p * GROUP
    near, far, diag = first + near_spot, first + far_spot, first + diag_spot
    rows = a_ref.shape[0]
    rank = pick_a.shape[0]
    width, hidden = pick_a.shape[1], pick_b.shape[1]
    half_a, half_b = width // 2, hidden // 2
    tokens = g.shape[0]
    slots = rows // rank
    f32, low = jnp.float32, jnp.bfloat16
    chunks = layout(width, hidden)
    count = len(chunks)

    def remote(src, dst, send, recv, seq_at, tp_at=mine):
        return pltpu.make_async_remote_copy(
            src_ref=src, dst_ref=dst, send_sem=send, recv_sem=recv,
            device_id=(seq_at, tp_at), device_id_type=MESH,
        )

    def at(index, step, size=None):
        return pl.ds(pl.multiple_of(index * step, step), step if size is None else size)

    def half_cols(chunk, which_half):
        which, _, start, size, _ = chunk
        half = half_a if which == "a" else half_b
        return pl.ds(pl.multiple_of(which_half * half + start, 128), size)

    def span(chunk):
        return pl.ds(chunk[4], chunk[3])

    def when(cond, body):
        if cond is True:
            body()
        else:
            pl.when(cond)(body)

    pending = []
    tick = [0]

    def send(copy, cond=True):
        copy.start()
        pending.append((tick[0], cond, copy))

    def drain(before):
        while pending and pending[0][0] < before:
            _, cond, copy = pending.pop(0)
            when(cond, copy.wait_send)

    local = [
        pltpu.make_async_copy(a_ref.at[:, at(core, half_a)], raw.at[at(spot, rows), pl.ds(0, half_a)], local_sem.at[0]),
        pltpu.make_async_copy(b_ref.at[:, at(core, half_b)], raw.at[at(spot, rows), pl.ds(half_a, half_b)], local_sem.at[1]),
        pltpu.make_async_copy(x_ref.at[:, at(mine, width)], xt.at[mine], local_sem.at[2]),
        pltpu.make_async_copy(g_ref, g, local_sem.at[3]),
    ]
    for copy in local:
        copy.start()
    adapter = adapter_ref[0]
    home = home_ref[adapter]
    id_row = lax.broadcasted_iota(jnp.int32, ids.shape[1:], 0)
    ids[me] = jnp.where(id_row == 0, adapter, home)
    others = [lax.rem(p + d, planes) for d in range(1, planes)]
    greet(n, tp, me, mine, [near, far, diag] + [q * GROUP + spot for q in others])
    for partner in (near, far, diag):
        send(remote(ids.at[me], ids.at[me], id_send.at[0], id_recv.at[planes], partner))
    pending.clear()

    factor_kind = [DOWN_FACTOR[i] if w == "a" else UP_FACTOR[i] for w, i, *_ in chunks]
    term_kind = [DOWN_GRADIENT[i] if w == "a" else UP_GRADIENT[i] for w, i, *_ in chunks]

    def x_first(kind):
        return kind in "xX"

    def relayed(kind):
        return kind in "xz"

    pairs = planes // 2
    pair = p // 2
    partner = p + 1 - 2 * lax.rem(p, 2)
    other_pairs = [lax.rem(pair + d, pairs) for d in range(1, pairs)]

    def inner(other):
        return 2 * other + (other < pair).astype(jnp.int32)

    def seat(plane):
        return plane * GROUP + spot

    def factor(chunk):
        return a_ref if chunk[0] == "a" else b_ref

    def picked(chunk):
        return pick_a if chunk[0] == "a" else pick_b

    raw_copies = {}

    def raw_out(j):
        chunk = chunks[j]
        own, sp = at(spot, rows), span(chunk)
        there, here = factor(chunk).at[:, half_cols(chunk, 1 - core)], factor(chunk).at[:, half_cols(chunk, core)]
        routes = [(there, near), (here, far), (there, diag)][:3 if x_first(factor_kind[j]) else 1]
        for src, to in routes:
            remote(src, raw.at[own, sp], raw_send.at[j], raw_recv.at[j], to).start()
        everything = raw.at[pl.ds(0, len(routes) * rows), sp]
        raw_copies[j] = remote(everything, everything, raw_send.at[j], raw_recv.at[j], near)
        pending.append((tick[0], True, raw_copies[j]))

    for j in range(min(AHEAD, count)):
        raw_out(j)
    x_copies = []
    for d in range(1, tp):
        peer = lax.rem(mine + d, tp)
        x_copies.append(remote(x_ref.at[:, at(peer, width)], xt.at[mine], x_send.at[d], x_recv.at[d], me, peer))
        x_copies[-1].start()
    for copy in local:
        copy.wait()
    plane_ids = ids.at[pl.ds(first, GROUP - 1)]
    remote(plane_ids, plane_ids, id_send.at[0], id_recv.at[planes], near).wait()

    def id_hop(source, to, sends):
        block = ids.at[at(source, GROUP)]
        return remote(block, block, sends, id_recv.at[source], to)

    for q in others:
        id_hop(p, q * GROUP + spot, id_send.at[1]).start()
    for q in others:
        id_hop(q, near, id_send.at[1]).wait_recv()
    other_ids = ids.at[pl.ds(0, GROUP * (planes - 1))]
    remote(other_ids, other_ids, id_send.at[1], id_recv.at[0], near).wait_send()

    def wanted(block, which, shape):
        return jnp.broadcast_to(ids[block, which:which + 1, 0:1], shape)

    def selector(spots, base, depth):
        shape = (rank, depth)
        row_at, col_at = lax.broadcasted_iota(jnp.int32, shape, 0), lax.broadcasted_iota(jnp.int32, shape, 1)
        found = []
        for q in range(planes):
            for s in spots:
                local_id = wanted(q * GROUP + s, 0, shape) - base
                found.append((col_at == local_id * rank + row_at).astype(f32))
        return jnp.concatenate(found, axis=0).astype(low)

    pick_x = selector([side * 2, side * 2 + 1], first * slots, GROUP * rows)
    pick_z = selector(list(range(GROUP)), (first + side * 2) * slots, 2 * rows)

    def placement(owner):
        shape = (rows, n * rank)
        row_at, col_at = lax.broadcasted_iota(jnp.int32, shape, 0), lax.broadcasted_iota(jnp.int32, shape, 1)
        target = jnp.full(shape, -1, jnp.int32)
        for block in range(n):
            begin = block * rank
            here = (wanted(block, 1, shape) - owner * slots) * rank + col_at - begin
            target = jnp.where((col_at >= begin) & (col_at < begin + rank), here, target)
        return (target == row_at).astype(f32).astype(low)

    place = jnp.concatenate([placement(me), placement(near)], axis=0)

    def factor_rows(j):
        return 2 * rank if x_first(factor_kind[j]) else GROUP * rank

    def select(j):
        sp, kind = span(chunks[j]), factor_kind[j]
        if j + AHEAD < count:
            raw_out(j + AHEAD)
        raw_copies[j].wait_recv()
        if x_first(kind):
            got = jnp.dot(pick_x, raw[:, sp], preferred_element_type=f32)
        else:
            got = jnp.dot(pick_z, raw[at(side, 2 * rows), sp], preferred_element_type=f32)
        depth = factor_rows(j)
        chosen[:, pl.ds(0, depth), sp] = got.astype(low).reshape(planes, depth, got.shape[1])

    def each_plane(body):
        for v in range(planes):
            pl.when(p == v)(functools.partial(body, v))

    def beyond(v):
        return pl.ds(v + 1, planes - 1 - v) if v % 2 == 0 else pl.ds(0, v)

    def plane_copies(j, count):
        block = far_land.at[pl.ds(0, count), pl.ds(0, factor_rows(j)), span(chunks[j])]
        return remote(block, block, plane_send.at[j], plane_recv.at[j], near)

    def send_plane(j, q):
        rest, sp = pl.ds(0, factor_rows(j)), span(chunks[j])
        remote(chosen.at[q, rest, sp], far_land.at[p, rest, sp], plane_send.at[j], plane_recv.at[j], seat(q)).start()

    def hop(j):
        if not relayed(factor_kind[j]):
            for q in others:
                send_plane(j, q)
            pending.append((tick[0], True, plane_copies(j, planes - 1)))
            return
        rest, sp = pl.ds(0, factor_rows(j)), span(chunks[j])

        def copy(v):
            part_of = beyond(v)
            return remote(
                chosen.at[part_of, rest, sp], land.at[part_of, rest, sp], hop_send.at[j], hop_recv.at[j], seat(partner)
            )

        each_plane(lambda v: copy(v).start())
        for v in range(planes):
            pending.append((tick[0], p == v, copy(v)))

    def relay(j):
        if not relayed(factor_kind[j]):
            return
        rest, sp = pl.ds(0, factor_rows(j)), span(chunks[j])

        def body(v):
            got = pl.ds(v, planes - v) if v % 2 else pl.ds(0, v + 1)
            here = land.at[got, rest, sp]
            remote(here, here, hop_send.at[j], hop_recv.at[j], near).wait_recv()
            chosen[got, rest, sp] = chosen[got, rest, sp] + land[got, rest, sp]
            for q in range(v + 1, planes) if v % 2 else range(v):
                send_plane(j, q)

        each_plane(body)
        for v in range(planes):
            sent = planes - 1 - v if v % 2 else v
            if sent:
                pending.append((tick[0], p == v, plane_copies(j, sent)))

    fin_copies = {}

    def final(j):
        chunk, depth = chunks[j], factor_rows(j)
        sp = span(chunk)
        rest = pl.ds(0, depth)
        sources = [inner(other) for other in other_pairs] if relayed(factor_kind[j]) else others
        if sources:
            plane_copies(j, len(sources)).wait_recv()
            total = chosen[p, rest, sp]
            for q in sources:
                total = total + far_land[q, rest, sp]
            chosen[p, rest, sp] = total
        target = picked(chunk)
        mine_cols = half_cols(chunk, core)
        if x_first(factor_kind[j]):
            fin_copies[j] = remote(
                chosen.at[p, at(1 - core, rank), sp], target.at[:, mine_cols], fin_send.at[j], fin_recv.at[j], near
            )
            fin_copies[j].start()
            target[:, mine_cols] = chosen[p, at(core, rank), sp]
        else:
            for k, (peer, peer_spot) in enumerate(((near, near_spot), (far, far_spot), (diag, diag_spot))):
                remote(chosen.at[p, at(peer_spot, rank), sp], fin.at[k, :, sp], fin_send.at[j], fin_recv.at[j], peer).start()
            fin_copies[j] = remote(fin.at[:, :, sp], fin.at[:, :, sp], fin_send.at[j], fin_recv.at[j], near)
        pending.append((tick[0], True, fin_copies[j]))

    def settle(j):
        chunk = chunks[j]
        sp = span(chunk)
        fin_copies[j].wait_recv()
        if not x_first(factor_kind[j]):
            target = picked(chunk)
            target[:, half_cols(chunk, core)] = chosen[p, at(spot, rank), sp] + fin[1, :, sp]
            target[:, half_cols(chunk, 1 - core)] = fin[0, :, sp] + fin[2, :, sp]

    def outer(left, right):
        return lax.dot_general(left, right, (((1,), (1,)), ((), ())), preferred_element_type=f32)

    part_copies = []
    lane = lax.broadcasted_iota(jnp.int32, (1, tokens), 1)
    alive = (lane < live_ref[0]).astype(f32)

    def share(which, value):
        part[which, 0] = value
        for d in range(1, tp):
            copy = remote(
                part.at[which, 0], part.at[which, d], part_send.at[which, d], part_recv.at[which, d],
                me, lax.rem(mine + d, tp),
            )
            send(copy)
            part_copies.append(copy)

    def collect(which):
        value = part[which, 0]
        for d in range(1, tp):
            part_copies[which * (tp - 1) + d - 1].wait_recv()
            value = value + part[which, d]
        return value * alive

    lead_copies = {}

    def lead(j, left, right, scale):
        chunk = chunks[j]
        sp, own = span(chunk), at(me, rank)

        def term(which_half):
            value = jnp.dot(left, right(half_cols(chunk, which_half)), preferred_element_type=f32)
            return (scale * value if scale is not None else value).astype(low)

        spare[:, sp] = term(1 - core)
        remote(spare.at[:, sp], terms.at[own, sp], lead_send.at[j], lead_recv.at[j], near).start()
        if not x_first(term_kind[j]):
            remote(spare.at[:, sp], terms.at[own, sp], lead_send.at[j], lead_recv.at[j], diag).start()
        terms[own, sp] = term(core)
        if not x_first(term_kind[j]):
            remote(terms.at[own, sp], terms.at[own, sp], lead_send.at[j], lead_recv.at[j], far).start()
        everything = terms.at[pl.ds(0, (1 if x_first(term_kind[j]) else GROUP - 1) * rank), sp]
        lead_copies[j] = remote(everything, everything, lead_send.at[j], lead_recv.at[j], near)
        pending.append((tick[0], True, lead_copies[j]))

    def group_rows(j, plane, other_side=False):
        if not x_first(term_kind[j]):
            return at(plane, GROUP * rank)
        return at(plane * 2 + (1 - side if other_side else side), 2 * rank)

    def term_copy(j, plane, sends, to):
        block = terms.at[group_rows(j, plane), span(chunks[j])]
        return remote(block, block, sends.at[j], go_recv.at[j, plane], to)

    def cross_copy(j, plane):
        block = terms.at[group_rows(j, plane), span(chunks[j])]
        return remote(block, block, cross_send.at[j], cross_recv.at[j], far)

    def crossed(j):
        everything = terms.at[pl.ds(0, planes * 2 * rank), span(chunks[j])]
        return remote(everything, everything, cross_send.at[j], cross_recv.at[j], far)

    def spread(j):
        lead_copies[j].wait_recv()
        targets = [partner] + [inner(other) for other in other_pairs] if relayed(term_kind[j]) else others
        for q in targets:
            term_copy(j, p, go_send, seat(q)).start()
        if x_first(term_kind[j]):
            cross_copy(j, p).start()
        pending.append((tick[0], True, term_copies(j, go_send, len(targets))))

    def term_copies(j, sends, number):
        block = terms.at[pl.ds(0, number * (2 if x_first(term_kind[j]) else GROUP) * rank), span(chunks[j])]
        return remote(block, block, sends.at[j], go_recv.at[j, 0], near)

    def arrive(j, q):
        term_copy(j, q, go_send, near).wait_recv()
        if x_first(term_kind[j]):
            cross_copy(j, q).start()

    def pass_on(j):
        if not relayed(term_kind[j]):
            for q in others:
                arrive(j, q)
            return
        arrive(j, partner)

        def body(v):
            for q in range(v) if v % 2 == 0 else range(planes - 1, v, -1):
                term_copy(j, q, go_send, near).wait_recv()
                term_copy(j, q, pass_send, seat(partner)).start()
                if x_first(term_kind[j]):
                    cross_copy(j, q).start()

        each_plane(body)
        for v in range(planes):
            passed = v if v % 2 == 0 else planes - 1 - v
            if passed:
                pending.append((tick[0], p == v, term_copies(j, pass_send, passed)))

    def gather(j):
        if relayed(term_kind[j]):

            def body(v):
                for q in range(v + 2, planes) if v % 2 == 0 else range(v - 2, -1, -1):
                    arrive(j, q)

            each_plane(body)
        if x_first(term_kind[j]):
            pending.append((tick[0], True, crossed(j)))

    out_copies = {}

    def finish(j):
        chunk = chunks[j]
        sp, cols = span(chunk), half_cols(chunk, core)
        if x_first(term_kind[j]):
            crossed(j).wait_recv()
        out = grad_a if chunk[0] == "a" else grad_b
        total = jnp.dot(place, terms[:, sp], preferred_element_type=f32)
        placed[:, sp] = total[rows:]
        out_copies[j] = remote(placed.at[:, sp], out.at[:, cols], out_send.at[j], out_recv.at[j], near)
        send(out_copies[j])
        out[:, cols] = total[:rows]

    state = {}

    def start_down():
        for copy in x_copies:
            copy.wait()
        share(0, outer(pick_a[...], xt[...].reshape(tokens, width)))

    def finish_down():
        down = collect(0).astype(low)
        state["down"] = down
        state["down_t"] = down.T

    def add_back(j):
        total = state.get("back")
        for h in (core, 1 - core):
            cols = half_cols(chunks[j], h)
            value = outer(pick_b[:, cols], g[:, cols])
            total = value if total is None else total + value
        state["back"] = total

    def output(j):
        for h in (core, 1 - core):
            cols = half_cols(chunks[j], h)
            value = jnp.dot(state["down_t"], pick_b[:, cols], preferred_element_type=f32)
            out_ref[:, cols] = (adapter_scale * value).astype(low)

    def start_back():
        share(1, state["back"])

    gx_copies = []

    def finish_back():
        back = adapter_scale * collect(1)
        state["back_low"] = back.astype(low)
        state["back_t"] = back.T.astype(low)

    def input_gradient():
        gx[...] = jnp.dot(state["back_t"], pick_a[...], preferred_element_type=f32).astype(low).reshape(gx.shape)
        for d in range(1, tp):
            peer = lax.rem(mine + d, tp)
            gx_copies.append(remote(gx.at[peer], x_out.at[:, at(mine, width)], gx_send.at[d], gx_recv.at[d], me, peer))
            gx_copies[-1].start()
        x_out[:, at(mine, width)] = gx[mine]

    events = []

    def plan(when_at, order, body):
        events.append((when_at, order, len(events), body))

    downs = [j for j in range(count) if chunks[j][0] == "a"]
    ups = [j for j in range(count) if chunks[j][0] == "b"]
    def settled_at(j):
        return j + (RELAY + LAND if relayed(factor_kind[j]) else LAND) + NEAR

    for j in range(count):
        plan(j, 5, functools.partial(select, j))
        plan(j, 5, functools.partial(hop, j))
        plan(j + RELAY, 4, functools.partial(relay, j))
        plan(settled_at(j) - NEAR, 3, functools.partial(final, j))
        plan(settled_at(j), 2, functools.partial(settle, j))
        if j in ups:
            plan(settled_at(j), 2, functools.partial(add_back, j))
    ready = max(settled_at(j) for j in downs)
    plan(ready, 2, start_down)
    plan(ready + SHARE, 1, finish_down)

    def chain(j, begin, left, right, scale):
        plan(begin, 6, lambda: lead(j, state[left], right, scale))
        arrived = begin + LEAD + SPREAD
        plan(begin + LEAD, 7, functools.partial(spread, j))
        plan(arrived, 8, functools.partial(pass_on, j))
        if relayed(term_kind[j]):
            arrived += SPREAD
        plan(arrived, 9, functools.partial(gather, j))
        if x_first(term_kind[j]):
            arrived += CROSS
        plan(arrived, 10, functools.partial(finish, j))

    for i, j in enumerate(ups):
        plan(max(ready + SHARE, settled_at(j)) + 2, 11, functools.partial(output, j))
        chain(j, ready + SHARE + i * PACE // 4, "down", lambda cols: g[:, cols], adapter_scale)
    whole = max(settled_at(j) for j in ups)
    plan(whole, 2, start_back)
    plan(whole + SHARE, 1, finish_back)
    for i, j in enumerate(downs):
        chain(j, whole + SHARE, "back_low", lambda cols: xt[:, :, cols].reshape(tokens, cols.size), None)
    plan(whole + SHARE, 12, input_gradient)
    events.sort(key=lambda event: event[:3])
    for i, event in enumerate(events):
        tick[0] = i
        drain(i - LAG)
        event[3]()
    for j in ups + downs:
        out_copies[j].wait_recv()
    for copy in gx_copies:
        copy.wait()
    drain(tick[0] + 1)


def step(n, tp, a, b, x, g, adapter, live, home):
    slots, rank, width = a.shape
    hidden = b.shape[2]
    rows = x.shape[0]
    tokens = g.shape[0]
    planes = n // GROUP
    cuts = len(layout(width, hidden))
    own = slots * rank
    each = (width + hidden) // 2
    low, f32 = jnp.bfloat16, jnp.float32
    dma = pltpu.SemaphoreType.DMA
    hbm = pl.BlockSpec(memory_space=pltpu.HBM)
    inside = pl.BlockSpec(memory_space=VMEM)
    scalar = pl.BlockSpec(memory_space=SMEM)
    lists = [dma((cuts,)) for _ in range(12)]
    results = ((tokens, hidden), low), ((own, width), f32), ((own, hidden), f32), ((rows, tp * width), low)
    held = pl.pallas_call(
        functools.partial(step_kernel, n, tp),
        out_shape=tuple(VMEM(*result) for result in results),
        in_specs=[hbm] * 4 + [scalar] * 3,
        out_specs=(inside,) * 4,
        scratch_shapes=[
            VMEM((rank, width), low), VMEM((rank, hidden), low), VMEM((GROUP * own, each), low),
            VMEM((planes, GROUP * rank, each), low),
            VMEM((planes, GROUP * rank, each), low), VMEM((planes, GROUP * rank, each), low),
            VMEM((3, rank, each), low), VMEM((n * rank, each), low), VMEM((rank, each), low), VMEM((own, each), f32),
            VMEM((tp, rows, width), low), VMEM((tokens, hidden), low),
            VMEM((n, 2, 128), jnp.int32), VMEM((2, tp, rank, tokens), f32), VMEM((tp, rows, width), low),
            *lists, dma((cuts, planes)), dma((cuts,)), dma((cuts,)), dma((cuts,)), dma((cuts,)),
            dma((3,)), dma((planes + 1,)), dma((tp,)), dma((tp,)), dma((2, tp)), dma((2, tp)),
            dma((tp,)), dma((tp,)), dma((4,)),
        ],
        compiler_params=pltpu.CompilerParams(
            collective_id=0, has_side_effects=True, vmem_limit_bytes=56 * 1024 * 1024
        ),
    )(a.reshape(own, width), b.reshape(own, hidden), x, g, adapter, live, home)
    anywhere = pl.BlockSpec(memory_space=pl.ANY)
    return pl.pallas_call(
        store_kernel,
        out_shape=tuple(jax.ShapeDtypeStruct(*result) for result in results),
        in_specs=[inside] * len(results),
        out_specs=(anywhere,) * len(results),
        scratch_shapes=[dma((len(results), STORES))],
        compiler_params=pltpu.CompilerParams(vmem_limit_bytes=1024 * 1024),
    )(*[pltpu.with_memory_space_constraint(value, VMEM) for value in held])


def store_kernel(*refs):
    sems = refs[-1]
    number = len(refs) // 2
    copies = []
    for i in range(number):
        rows = refs[i].shape[0] // STORES
        for k in range(STORES):
            part = pl.ds(k * rows, rows)
            copies.append(pltpu.make_async_copy(refs[i].at[part], refs[number + i].at[part], sems.at[i, k]))
    for copy in copies:
        copy.start()
    for copy in copies:
        copy.wait()


def per_device(
    normed_input,
    output_gradient,
    adapter_down,
    adapter_up,
    adapter_of_block,
    live_per_block,
    adapter_home_row,
):
    n, tp = lax.axis_size("seq"), lax.axis_size("tp")
    slots, rank, width = adapter_down.shape
    hidden = adapter_up.shape[2]
    out, grad_a, grad_b, gx = step(
        n, tp, adapter_down, adapter_up, normed_input, output_gradient,
        adapter_of_block, live_per_block, adapter_home_row,
    )
    return (out, gx, grad_a.reshape(slots, rank, width), grad_b.reshape(slots, rank, hidden))


def solution(mesh):
    placed = (
        P(("seq", "tp"), None),
        P("seq", "tp"),
        P("seq", None, "tp"),
        P("seq", None, "tp"),
        P("seq"),
        P("seq"),
        P(),
    )
    return jax.shard_map(
        per_device,
        mesh=mesh,
        in_specs=placed,
        out_specs=(
            P("seq", "tp"),
            P(("seq", "tp"), None),
            P("seq", None, "tp"),
            P("seq", None, "tp"),
        ),
        check_vma=False,
    )
```

```python
import functools

import jax
import jax.numpy as jnp
from jax import lax
from jax.experimental import pallas as pl
from jax.experimental.pallas import tpu as pltpu
from jax.sharding import PartitionSpec as P

adapter_scale = 2.0
GROUP = 4
MESH = pl.DeviceIdType.MESH
VMEM = pltpu.VMEM
SMEM = pltpu.SMEM

DOWN_FACTOR, UP_FACTOR = "XX", "xxzXxxx"
UP_GRADIENT, DOWN_GRADIENT = "xxxxxxX", "XZ"
DOWN_SHARES, UP_SHARES = (4, 4), (5, 4, 2, 4, 5, 5, 3)
RELAY, LAND, NEAR, SHARE, LEAD, SPREAD, CROSS = 2, 2, 1, 1, 1, 2, 2
AHEAD, LAG, PACE = 6, 45, 5
STORES = 1


def pieces(width, shares):
    tiles, total, seen, start, out = width // 128, sum(shares), 0, 0, []
    for i, share in enumerate(shares):
        seen += share
        end = (2 * seen * tiles + total) // (2 * total)
        if end > start:
            out.append((i, start * 128, (end - start) * 128))
        start = end
    return out


def layout(width, hidden):
    halves = ("a", 0, width // 2, DOWN_SHARES), ("b", width // 2, hidden // 2, UP_SHARES)
    return [
        (which, i, start, size, base + start)
        for which, base, half, shares in halves for i, start, size in pieces(half, shares)
    ]


def greet(n, tp, me, mine, partners):
    barrier = pltpu.get_barrier_semaphore()

    def signal(seq_at, tp_at):
        pl.semaphore_signal(barrier, inc=1, device_id=(seq_at, tp_at), device_id_type=MESH)

    for partner in partners:
        signal(partner, mine)
    for d in range(1, tp):
        signal(me, lax.rem(mine + d, tp))
    pl.semaphore_wait(barrier, len(partners) + tp - 1)


def step_kernel(
    n, tp, a_ref, b_ref, x_ref, g_ref, adapter_ref, live_ref, home_ref,
    out_ref, grad_a, grad_b, x_out,
    pick_a, pick_b, raw, chosen, land, far_land, fin, terms, spare, placed, xt, g, ids, part, gx,
    raw_send, raw_recv, hop_send, hop_recv, plane_send, plane_recv, fin_send, fin_recv,
    lead_send, lead_recv, go_send, pass_send, go_recv, cross_send, cross_recv, out_send, out_recv,
    id_send, id_recv, x_send, x_recv, part_send, part_recv, gx_send, gx_recv, local_sem,
):
    me, mine = lax.axis_index("seq"), lax.axis_index("tp")
    planes = n // GROUP
    p, spot = me // GROUP, lax.rem(me, GROUP)
    side, core = spot // 2, lax.rem(spot, 2)
    near_spot, far_spot = spot + 1 - 2 * core, spot + 2 - 4 * side
    diag_spot = far_spot + 1 - 2 * core
    first = p * GROUP
    near, far, diag = first + near_spot, first + far_spot, first + diag_spot
    rows = a_ref.shape[0]
    rank = pick_a.shape[0]
    width, hidden = pick_a.shape[1], pick_b.shape[1]
    half_a, half_b = width // 2, hidden // 2
    tokens = g.shape[0]
    slots = rows // rank
    f32, low = jnp.float32, jnp.bfloat16
    chunks = layout(width, hidden)
    count = len(chunks)

    def remote(src, dst, send, recv, seq_at, tp_at=mine):
        return pltpu.make_async_remote_copy(
            src_ref=src, dst_ref=dst, send_sem=send, recv_sem=recv,
            device_id=(seq_at, tp_at), device_id_type=MESH,
        )

    def at(index, step, size=None):
        return pl.ds(pl.multiple_of(index * step, step), step if size is None else size)

    def half_cols(chunk, which_half):
        which, _, start, size, _ = chunk
        half = half_a if which == "a" else half_b
        return pl.ds(pl.multiple_of(which_half * half + start, 128), size)

    def span(chunk):
        return pl.ds(chunk[4], chunk[3])

    def when(cond, body):
        if cond is True:
            body()
        else:
            pl.when(cond)(body)

    pending = []
    tick = [0]

    def send(copy, cond=True):
        copy.start()
        pending.append((tick[0], cond, copy))

    def drain(before):
        while pending and pending[0][0] < before:
            _, cond, copy = pending.pop(0)
            when(cond, copy.wait_send)

    local = [
        pltpu.make_async_copy(a_ref.at[:, at(core, half_a)], raw.at[at(spot, rows), pl.ds(0, half_a)], local_sem.at[0]),
        pltpu.make_async_copy(b_ref.at[:, at(core, half_b)], raw.at[at(spot, rows), pl.ds(half_a, half_b)], local_sem.at[1]),
        pltpu.make_async_copy(x_ref.at[:, at(mine, width)], xt.at[mine], local_sem.at[2]),
        pltpu.make_async_copy(g_ref, g, local_sem.at[3]),
    ]
    for copy in local:
        copy.start()
    adapter = adapter_ref[0]
    home = home_ref[adapter]
    id_row = lax.broadcasted_iota(jnp.int32, ids.shape[1:], 0)
    ids[me] = jnp.where(id_row == 0, adapter, home)
    others = [lax.rem(p + d, planes) for d in range(1, planes)]
    greet(n, tp, me, mine, [near, far, diag] + [q * GROUP + spot for q in others])
    for partner in (near, far, diag):
        send(remote(ids.at[me], ids.at[me], id_send.at[0], id_recv.at[planes], partner))
    pending.clear()

    factor_kind = [DOWN_FACTOR[i] if w == "a" else UP_FACTOR[i] for w, i, *_ in chunks]
    term_kind = [DOWN_GRADIENT[i] if w == "a" else UP_GRADIENT[i] for w, i, *_ in chunks]

    def x_first(kind):
        return kind in "xX"

    def relayed(kind):
        return kind in "xz"

    pairs = planes // 2
    pair = p // 2
    partner = p + 1 - 2 * lax.rem(p, 2)
    other_pairs = [lax.rem(pair + d, pairs) for d in range(1, pairs)]

    def inner(other):
        return 2 * other + (other < pair).astype(jnp.int32)

    def seat(plane):
        return plane * GROUP + spot

    def factor(chunk):
        return a_ref if chunk[0] == "a" else b_ref

    def picked(chunk):
        return pick_a if chunk[0] == "a" else pick_b

    raw_copies = {}

    def raw_out(j):
        chunk = chunks[j]
        own, sp = at(spot, rows), span(chunk)
        there, here = factor(chunk).at[:, half_cols(chunk, 1 - core)], factor(chunk).at[:, half_cols(chunk, core)]
        routes = [(there, near), (here, far), (there, diag)][:3 if x_first(factor_kind[j]) else 1]
        for src, to in routes:
            remote(src, raw.at[own, sp], raw_send.at[j], raw_recv.at[j], to).start()
        everything = raw.at[pl.ds(0, len(routes) * rows), sp]
        raw_copies[j] = remote(everything, everything, raw_send.at[j], raw_recv.at[j], near)
        pending.append((tick[0], True, raw_copies[j]))

    for j in range(min(AHEAD, count)):
        raw_out(j)
    x_copies = []
    for d in range(1, tp):
        peer = lax.rem(mine + d, tp)
        x_copies.append(remote(x_ref.at[:, at(peer, width)], xt.at[mine], x_send.at[d], x_recv.at[d], me, peer))
        x_copies[-1].start()
    for copy in local:
        copy.wait()
    plane_ids = ids.at[pl.ds(first, GROUP - 1)]
    remote(plane_ids, plane_ids, id_send.at[0], id_recv.at[planes], near).wait()

    def id_hop(source, to, sends):
        block = ids.at[at(source, GROUP)]
        return remote(block, block, sends, id_recv.at[source], to)

    for q in others:
        id_hop(p, q * GROUP + spot, id_send.at[1]).start()
    for q in others:
        id_hop(q, near, id_send.at[1]).wait_recv()
    other_ids = ids.at[pl.ds(0, GROUP * (planes - 1))]
    remote(other_ids, other_ids, id_send.at[1], id_recv.at[0], near).wait_send()

    def wanted(block, which, shape):
        return jnp.broadcast_to(ids[block, which:which + 1, 0:1], shape)

    def selector(spots, base, depth):
        shape = (rank, depth)
        row_at, col_at = lax.broadcasted_iota(jnp.int32, shape, 0), lax.broadcasted_iota(jnp.int32, shape, 1)
        found = []
        for q in range(planes):
            for s in spots:
                local_id = wanted(q * GROUP + s, 0, shape) - base
                found.append((col_at == local_id * rank + row_at).astype(f32))
        return jnp.concatenate(found, axis=0).astype(low)

    pick_x = selector([side * 2, side * 2 + 1], first * slots, GROUP * rows)
    pick_z = selector(list(range(GROUP)), (first + side * 2) * slots, 2 * rows)

    def placement(owner):
        shape = (rows, n * rank)
        row_at, col_at = lax.broadcasted_iota(jnp.int32, shape, 0), lax.broadcasted_iota(jnp.int32, shape, 1)
        target = jnp.full(shape, -1, jnp.int32)
        for block in range(n):
            begin = block * rank
            here = (wanted(block, 1, shape) - owner * slots) * rank + col_at - begin
            target = jnp.where((col_at >= begin) & (col_at < begin + rank), here, target)
        return (target == row_at).astype(f32).astype(low)

    place = jnp.concatenate([placement(me), placement(near)], axis=0)

    def factor_rows(j):
        return 2 * rank if x_first(factor_kind[j]) else GROUP * rank

    def select(j):
        sp, kind = span(chunks[j]), factor_kind[j]
        if j + AHEAD < count:
            raw_out(j + AHEAD)
        raw_copies[j].wait_recv()
        if x_first(kind):
            got = jnp.dot(pick_x, raw[:, sp], preferred_element_type=f32)
        else:
            got = jnp.dot(pick_z, raw[at(side, 2 * rows), sp], preferred_element_type=f32)
        depth = factor_rows(j)
        chosen[:, pl.ds(0, depth), sp] = got.astype(low).reshape(planes, depth, got.shape[1])

    def each_plane(body):
        for v in range(planes):
            pl.when(p == v)(functools.partial(body, v))

    def beyond(v):
        return pl.ds(v + 1, planes - 1 - v) if v % 2 == 0 else pl.ds(0, v)

    def plane_copies(j, count):
        block = far_land.at[pl.ds(0, count), pl.ds(0, factor_rows(j)), span(chunks[j])]
        return remote(block, block, plane_send.at[j], plane_recv.at[j], near)

    def send_plane(j, q):
        rest, sp = pl.ds(0, factor_rows(j)), span(chunks[j])
        remote(chosen.at[q, rest, sp], far_land.at[p, rest, sp], plane_send.at[j], plane_recv.at[j], seat(q)).start()

    def hop(j):
        if not relayed(factor_kind[j]):
            for q in others:
                send_plane(j, q)
            pending.append((tick[0], True, plane_copies(j, planes - 1)))
            return
        rest, sp = pl.ds(0, factor_rows(j)), span(chunks[j])

        def copy(v):
            part_of = beyond(v)
            return remote(
                chosen.at[part_of, rest, sp], land.at[part_of, rest, sp], hop_send.at[j], hop_recv.at[j], seat(partner)
            )

        each_plane(lambda v: copy(v).start())
        for v in range(planes):
            pending.append((tick[0], p == v, copy(v)))

    def relay(j):
        if not relayed(factor_kind[j]):
            return
        rest, sp = pl.ds(0, factor_rows(j)), span(chunks[j])

        def body(v):
            got = pl.ds(v, planes - v) if v % 2 else pl.ds(0, v + 1)
            here = land.at[got, rest, sp]
            remote(here, here, hop_send.at[j], hop_recv.at[j], near).wait_recv()
            chosen[got, rest, sp] = chosen[got, rest, sp] + land[got, rest, sp]
            for q in range(v + 1, planes) if v % 2 else range(v):
                send_plane(j, q)

        each_plane(body)
        for v in range(planes):
            sent = planes - 1 - v if v % 2 else v
            if sent:
                pending.append((tick[0], p == v, plane_copies(j, sent)))

    fin_copies = {}

    def final(j):
        chunk, depth = chunks[j], factor_rows(j)
        sp = span(chunk)
        rest = pl.ds(0, depth)
        sources = [inner(other) for other in other_pairs] if relayed(factor_kind[j]) else others
        if sources:
            plane_copies(j, len(sources)).wait_recv()
            total = chosen[p, rest, sp]
            for q in sources:
                total = total + far_land[q, rest, sp]
            chosen[p, rest, sp] = total
        target = picked(chunk)
        mine_cols = half_cols(chunk, core)
        if x_first(factor_kind[j]):
            fin_copies[j] = remote(
                chosen.at[p, at(1 - core, rank), sp], target.at[:, mine_cols], fin_send.at[j], fin_recv.at[j], near
            )
            fin_copies[j].start()
            target[:, mine_cols] = chosen[p, at(core, rank), sp]
        else:
            for k, (peer, peer_spot) in enumerate(((near, near_spot), (far, far_spot), (diag, diag_spot))):
                remote(chosen.at[p, at(peer_spot, rank), sp], fin.at[k, :, sp], fin_send.at[j], fin_recv.at[j], peer).start()
            fin_copies[j] = remote(fin.at[:, :, sp], fin.at[:, :, sp], fin_send.at[j], fin_recv.at[j], near)
        pending.append((tick[0], True, fin_copies[j]))

    def settle(j):
        chunk = chunks[j]
        sp = span(chunk)
        fin_copies[j].wait_recv()
        if not x_first(factor_kind[j]):
            target = picked(chunk)
            target[:, half_cols(chunk, core)] = chosen[p, at(spot, rank), sp] + fin[1, :, sp]
            target[:, half_cols(chunk, 1 - core)] = fin[0, :, sp] + fin[2, :, sp]

    def outer(left, right):
        return lax.dot_general(left, right, (((1,), (1,)), ((), ())), preferred_element_type=f32)

    part_copies = []
    lane = lax.broadcasted_iota(jnp.int32, (1, tokens), 1)
    alive = (lane < live_ref[0]).astype(f32)

    def share(which, value):
        part[which, 0] = value
        for d in range(1, tp):
            copy = remote(
                part.at[which, 0], part.at[which, d], part_send.at[which, d], part_recv.at[which, d],
                me, lax.rem(mine + d, tp),
            )
            send(copy)
            part_copies.append(copy)

    def collect(which):
        value = part[which, 0]
        for d in range(1, tp):
            part_copies[which * (tp - 1) + d - 1].wait_recv()
            value = value + part[which, d]
        return value * alive

    lead_copies = {}

    def lead(j, left, right, scale):
        chunk = chunks[j]
        sp, own = span(chunk), at(me, rank)

        def term(which_half):
            value = jnp.dot(left, right(half_cols(chunk, which_half)), preferred_element_type=f32)
            return (scale * value if scale is not None else value).astype(low)

        spare[:, sp] = term(1 - core)
        remote(spare.at[:, sp], terms.at[own, sp], lead_send.at[j], lead_recv.at[j], near).start()
        if not x_first(term_kind[j]):
            remote(spare.at[:, sp], terms.at[own, sp], lead_send.at[j], lead_recv.at[j], diag).start()
        terms[own, sp] = term(core)
        if not x_first(term_kind[j]):
            remote(terms.at[own, sp], terms.at[own, sp], lead_send.at[j], lead_recv.at[j], far).start()
        everything = terms.at[pl.ds(0, (1 if x_first(term_kind[j]) else GROUP - 1) * rank), sp]
        lead_copies[j] = remote(everything, everything, lead_send.at[j], lead_recv.at[j], near)
        pending.append((tick[0], True, lead_copies[j]))

    def group_rows(j, plane, other_side=False):
        if not x_first(term_kind[j]):
            return at(plane, GROUP * rank)
        return at(plane * 2 + (1 - side if other_side else side), 2 * rank)

    def term_copy(j, plane, sends, to):
        block = terms.at[group_rows(j, plane), span(chunks[j])]
        return remote(block, block, sends.at[j], go_recv.at[j, plane], to)

    def cross_copy(j, plane):
        block = terms.at[group_rows(j, plane), span(chunks[j])]
        return remote(block, block, cross_send.at[j], cross_recv.at[j], far)

    def crossed(j):
        everything = terms.at[pl.ds(0, planes * 2 * rank), span(chunks[j])]
        return remote(everything, everything, cross_send.at[j], cross_recv.at[j], far)

    def spread(j):
        lead_copies[j].wait_recv()
        targets = [partner] + [inner(other) for other in other_pairs] if relayed(term_kind[j]) else others
        for q in targets:
            term_copy(j, p, go_send, seat(q)).start()
        if x_first(term_kind[j]):
            cross_copy(j, p).start()
        pending.append((tick[0], True, term_copies(j, go_send, len(targets))))

    def term_copies(j, sends, number):
        block = terms.at[pl.ds(0, number * (2 if x_first(term_kind[j]) else GROUP) * rank), span(chunks[j])]
        return remote(block, block, sends.at[j], go_recv.at[j, 0], near)

    def arrive(j, q):
        term_copy(j, q, go_send, near).wait_recv()
        if x_first(term_kind[j]):
            cross_copy(j, q).start()

    def pass_on(j):
        if not relayed(term_kind[j]):
            for q in others:
                arrive(j, q)
            return
        arrive(j, partner)

        def body(v):
            for q in range(v) if v % 2 == 0 else range(planes - 1, v, -1):
                term_copy(j, q, go_send, near).wait_recv()
                term_copy(j, q, pass_send, seat(partner)).start()
                if x_first(term_kind[j]):
                    cross_copy(j, q).start()

        each_plane(body)
        for v in range(planes):
            passed = v if v % 2 == 0 else planes - 1 - v
            if passed:
                pending.append((tick[0], p == v, term_copies(j, pass_send, passed)))

    def gather(j):
        if relayed(term_kind[j]):

            def body(v):
                for q in range(v + 2, planes) if v % 2 == 0 else range(v - 2, -1, -1):
                    arrive(j, q)

            each_plane(body)
        if x_first(term_kind[j]):
            pending.append((tick[0], True, crossed(j)))

    out_copies = {}

    def finish(j):
        chunk = chunks[j]
        sp, cols = span(chunk), half_cols(chunk, core)
        if x_first(term_kind[j]):
            crossed(j).wait_recv()
        out = grad_a if chunk[0] == "a" else grad_b
        total = jnp.dot(place, terms[:, sp], preferred_element_type=f32)
        placed[:, sp] = total[rows:]
        out_copies[j] = remote(placed.at[:, sp], out.at[:, cols], out_send.at[j], out_recv.at[j], near)
        send(out_copies[j])
        out[:, cols] = total[:rows]

    state = {}

    def start_down():
        for copy in x_copies:
            copy.wait()
        share(0, outer(pick_a[...], xt[...].reshape(tokens, width)))

    def finish_down():
        down = collect(0).astype(low)
        state["down"] = down
        state["down_t"] = down.T

    def add_back(j):
        total = state.get("back")
        for h in (core, 1 - core):
            cols = half_cols(chunks[j], h)
            value = outer(pick_b[:, cols], g[:, cols])
            total = value if total is None else total + value
        state["back"] = total

    def output(j):
        for h in (core, 1 - core):
            cols = half_cols(chunks[j], h)
            value = jnp.dot(state["down_t"], pick_b[:, cols], preferred_element_type=f32)
            out_ref[:, cols] = (adapter_scale * value).astype(low)

    def start_back():
        share(1, state["back"])

    gx_copies = []

    def finish_back():
        back = adapter_scale * collect(1)
        state["back_low"] = back.astype(low)
        state["back_t"] = back.T.astype(low)

    def input_gradient():
        gx[...] = jnp.dot(state["back_t"], pick_a[...], preferred_element_type=f32).astype(low).reshape(gx.shape)
        for d in range(1, tp):
            peer = lax.rem(mine + d, tp)
            gx_copies.append(remote(gx.at[peer], x_out.at[:, at(mine, width)], gx_send.at[d], gx_recv.at[d], me, peer))
            gx_copies[-1].start()
        x_out[:, at(mine, width)] = gx[mine]

    events = []

    def plan(when_at, order, body):
        events.append((when_at, order, len(events), body))

    downs = [j for j in range(count) if chunks[j][0] == "a"]
    ups = [j for j in range(count) if chunks[j][0] == "b"]
    def settled_at(j):
        return j + (RELAY + LAND if relayed(factor_kind[j]) else LAND) + NEAR

    for j in range(count):
        plan(j, 5, functools.partial(select, j))
        plan(j, 5, functools.partial(hop, j))
        plan(j + RELAY, 4, functools.partial(relay, j))
        plan(settled_at(j) - NEAR, 3, functools.partial(final, j))
        plan(settled_at(j), 2, functools.partial(settle, j))
        if j in ups:
            plan(settled_at(j), 2, functools.partial(add_back, j))
    ready = max(settled_at(j) for j in downs)
    plan(ready, 2, start_down)
    plan(ready + SHARE, 1, finish_down)

    def chain(j, begin, left, right, scale):
        plan(begin, 6, lambda: lead(j, state[left], right, scale))
        arrived = begin + LEAD + SPREAD
        plan(begin + LEAD, 7, functools.partial(spread, j))
        plan(arrived, 8, functools.partial(pass_on, j))
        if relayed(term_kind[j]):
            arrived += SPREAD
        plan(arrived, 9, functools.partial(gather, j))
        if x_first(term_kind[j]):
            arrived += CROSS
        plan(arrived, 10, functools.partial(finish, j))

    for i, j in enumerate(ups):
        plan(max(ready + SHARE, settled_at(j)) + 2, 11, functools.partial(output, j))
        chain(j, ready + SHARE + i * PACE // 4, "down", lambda cols: g[:, cols], adapter_scale)
    whole = max(settled_at(j) for j in ups)
    plan(whole, 2, start_back)
    plan(whole + SHARE, 1, finish_back)
    for i, j in enumerate(downs):
        chain(j, whole + SHARE, "back_low", lambda cols: xt[:, :, cols].reshape(tokens, cols.size), None)
    plan(whole + SHARE, 12, input_gradient)
    events.sort(key=lambda event: event[:3])
    for i, event in enumerate(events):
        tick[0] = i
        drain(i - LAG)
        event[3]()
    for j in ups + downs:
        out_copies[j].wait_recv()
    for copy in gx_copies:
        copy.wait()
    drain(tick[0] + 1)


def step(n, tp, a, b, x, g, adapter, live, home):
    slots, rank, width = a.shape
    hidden = b.shape[2]
    rows = x.shape[0]
    tokens = g.shape[0]
    planes = n // GROUP
    cuts = len(layout(width, hidden))
    own = slots * rank
    each = (width + hidden) // 2
    low, f32 = jnp.bfloat16, jnp.float32
    dma = pltpu.SemaphoreType.DMA
    hbm = pl.BlockSpec(memory_space=pltpu.HBM)
    inside = pl.BlockSpec(memory_space=VMEM)
    scalar = pl.BlockSpec(memory_space=SMEM)
    lists = [dma((cuts,)) for _ in range(12)]
    results = ((tokens, hidden), low), ((own, width), f32), ((own, hidden), f32), ((rows, tp * width), low)
    held = pl.pallas_call(
        functools.partial(step_kernel, n, tp),
        out_shape=tuple(VMEM(*result) for result in results),
        in_specs=[hbm] * 4 + [scalar] * 3,
        out_specs=(inside,) * 4,
        scratch_shapes=[
            VMEM((rank, width), low), VMEM((rank, hidden), low), VMEM((GROUP * own, each), low),
            VMEM((planes, GROUP * rank, each), low),
            VMEM((planes, GROUP * rank, each), low), VMEM((planes, GROUP * rank, each), low),
            VMEM((3, rank, each), low), VMEM((n * rank, each), low), VMEM((rank, each), low), VMEM((own, each), f32),
            VMEM((tp, rows, width), low), VMEM((tokens, hidden), low),
            VMEM((n, 2, 128), jnp.int32), VMEM((2, tp, rank, tokens), f32), VMEM((tp, rows, width), low),
            *lists, dma((cuts, planes)), dma((cuts,)), dma((cuts,)), dma((cuts,)), dma((cuts,)),
            dma((3,)), dma((planes + 1,)), dma((tp,)), dma((tp,)), dma((2, tp)), dma((2, tp)),
            dma((tp,)), dma((tp,)), dma((4,)),
        ],
        compiler_params=pltpu.CompilerParams(
            collective_id=0, has_side_effects=True, vmem_limit_bytes=56 * 1024 * 1024
        ),
    )(a.reshape(own, width), b.reshape(own, hidden), x, g, adapter, live, home)
    anywhere = pl.BlockSpec(memory_space=pl.ANY)
    return pl.pallas_call(
        store_kernel,
        out_shape=tuple(jax.ShapeDtypeStruct(*result) for result in results),
        in_specs=[inside] * len(results),
        out_specs=(anywhere,) * len(results),
        scratch_shapes=[dma((len(results), STORES))],
        compiler_params=pltpu.CompilerParams(vmem_limit_bytes=1024 * 1024),
    )(*[pltpu.with_memory_space_constraint(value, VMEM) for value in held])


def store_kernel(*refs):
    sems = refs[-1]
    number = len(refs) // 2
    copies = []
    for i in range(number):
        rows = refs[i].shape[0] // STORES
        for k in range(STORES):
            part = pl.ds(k * rows, rows)
            copies.append(pltpu.make_async_copy(refs[i].at[part], refs[number + i].at[part], sems.at[i, k]))
    for copy in copies:
        copy.start()
    for copy in copies:
        copy.wait()


def per_device(
    normed_input,
    output_gradient,
    adapter_down,
    adapter_up,
    adapter_of_block,
    live_per_block,
    adapter_home_row,
):
    n, tp = lax.axis_size("seq"), lax.axis_size("tp")
    slots, rank, width = adapter_down.shape
    hidden = adapter_up.shape[2]
    out, grad_a, grad_b, gx = step(
        n, tp, adapter_down, adapter_up, normed_input, output_gradient,
        adapter_of_block, live_per_block, adapter_home_row,
    )
    return (out, gx, grad_a.reshape(slots, rank, width), grad_b.reshape(slots, rank, hidden))


def solution(mesh):
    placed = (
        P(("seq", "tp"), None),
        P("seq", "tp"),
        P("seq", None, "tp"),
        P("seq", None, "tp"),
        P("seq"),
        P("seq"),
        P(),
    )
    return jax.shard_map(
        per_device,
        mesh=mesh,
        in_specs=placed,
        out_specs=(
            P("seq", "tp"),
            P(("seq", "tp"), None),
            P("seq", None, "tp"),
            P("seq", None, "tp"),
        ),
        check_vma=False,
    )
```
